512 devices in a mesh: row: 16 (over z, y_lo), col: 32 (over x, y_hi, core).
Axes of the slice: x: 4, y: 8 (y_hi: 4, y_lo: 2; y = y_hi * 2 + y_lo), z: 8, core: 2. Of those that a mesh axis runs over, the one named last changes fastest.
Arguments:
- green_blocks: bfloat16 [16, 32, 12, 2, 288, 288], P('row', 'col'), may hold values from -0.0625 to 0.0625
- slot_rows: int32 [16, 32, 12], P('row', 'col'), may hold values from 0 to 7, as said below
- slot_cols: int32 [16, 32, 12], P('row', 'col'), may hold values from 0 to 3
- slot_count: int32 [16, 32], P('row', 'col'), may hold values from 2 to 12, as said below
- cell_class: int32 [4, 32, 96], P(None, 'col'), may hold values from 0 to 15
- class_contrast: float32 [16, 2], replicated, may hold values from -0.6 to 0.6
- background: float32 [2, 32, 4, 32, 288], P(None, None, None, 'col'), may hold values from -6 to 6
Outputs:
- total_field: float32 [2, 32, 4, 32, 288], P(None, None, None, 'col')
The draws below stay inside these ranges and needn't reach their ends.
Inputs may be any that keep to these rules, and one draw needn't show every extreme that they name: slot_rows[r, c, s] and slot_cols[r, c, s] name different block pairs within one device's slots, and every slot, used or not, names a block in the upper triangle: (slot_rows // 2) * 32 + 2 r + slot_rows % 2 is at most slot_cols * 32 + c. Slots from slot_count[r, c] on are not used. `slot_count`: some device holds exactly 12 stored blocks.
All inputs are finite; a program needn't handle non-finite values.
Results may differ from the reference program's by a relative error of at most 0.0033.
Values may be sent and summed in bfloat16 or wider, within the bound.
A program may use at most 64 MiB of HBM per device.

```python
import jax
import jax.numpy as jnp
from jax import lax

BLOCK = 96
ENTRIES = 288
SOURCES = 32
COL_BLOCKS = 4
ROW_BLOCKS = 8
SLOTS = 12
CLASSES = 16
PRODUCTS = 3
GRID_ROWS = 16
STRIDE = 32
BLOCKS = 128


def pattern_tables(key):
    base = jax.random.fold_in(key, 11)
    key_score, key_first, key_second, key_full = jax.random.split(base, 4)
    pairs = ROW_BLOCKS * COL_BLOCKS
    local_row = jnp.arange(ROW_BLOCKS, dtype=jnp.int32)[None, None, :, None]
    local_col = jnp.arange(COL_BLOCKS, dtype=jnp.int32)[None, None, None, :]
    grid_row = jnp.arange(GRID_ROWS, dtype=jnp.int32)[:, None, None, None]
    grid_col = jnp.arange(STRIDE, dtype=jnp.int32)[None, :, None, None]
    block_row = local_row // 2 * STRIDE + 2 * grid_row + local_row % 2
    block_col = local_col * STRIDE + grid_col
    upper = (block_row <= block_col).reshape(GRID_ROWS, STRIDE, pairs)
    scores = jax.random.randint(key_score, (GRID_ROWS, STRIDE, pairs), 0, 1024) * 64 + jnp.arange(pairs, dtype=jnp.int32)
    scores = jnp.where(upper, scores, scores + 131072)
    order = jnp.argsort(scores, axis=-1, stable=True)[:, :, :SLOTS]
    rows_out = (order // COL_BLOCKS).astype(jnp.int32)
    cols_out = (order % COL_BLOCKS).astype(jnp.int32)
    first = jax.random.randint(key_first, (GRID_ROWS, STRIDE), 0, 11)
    second = jax.random.randint(key_second, (GRID_ROWS, STRIDE), 0, 11)
    counts = 2 + first * second * (SLOTS - 2) // 100
    chosen = jax.random.randint(key_full, (), 0, GRID_ROWS * STRIDE)
    flat = jnp.arange(GRID_ROWS * STRIDE, dtype=jnp.int32).reshape(GRID_ROWS, STRIDE)
    counts = jnp.where(flat == chosen, SLOTS, counts).astype(jnp.int32)
    return (rows_out, cols_out, counts)


def draw_slot_rows(key, part):
    return pattern_tables(key)[0]


def draw_slot_cols(key, part):
    return pattern_tables(key)[1]


def draw_slot_count(key, part):
    return pattern_tables(key)[2]


def with_ends(result, stream_key, least, high):
    place = [jax.random.randint(jax.random.fold_in(stream_key, axis), (), 0, length) for axis, length in enumerate(result.shape)]
    widest = result.shape.index(max(result.shape))
    neighbour = place[:widest] + [(place[widest] + 1) % result.shape[widest]] + place[widest + 1:]
    return result.at[tuple(place)].set(least).at[tuple(neighbour)].set(high)


def levels(own_key, dims, cuts, smallest, high):
    factor_of, own = 1.0, jax.random.fold_in(own_key, 6)
    for dim, blocks in cuts:
        heights = jnp.exp(jax.random.uniform(jax.random.fold_in(own, dim), (blocks,), jnp.float32, smallest / len(cuts), high / len(cuts)))
        factor_of = factor_of * jnp.repeat(heights, dims[dim] // blocks).reshape([-1 if axis == dim else 1 for axis in range(len(dims))])
    return factor_of


def centred(key, dims, spread, most, shards=(), kind=jnp.bfloat16):
    result = spread * jax.random.normal(key, dims, jnp.float32)
    if shards:
        result = result * levels(key, dims, shards, -0.22, 0.18)
    return jnp.clip(result, -most, most).astype(kind)


def setup_inputs(seed: int = 0) -> dict:
    arg_keys = jax.random.split(jax.random.key(seed), 8)
    green_blocks = centred(arg_keys[0], (GRID_ROWS, STRIDE, SLOTS, 2, ENTRIES, ENTRIES), (STRIDE * ENTRIES) ** -0.5, 0.0625, ((0, 16), (1, 32)))
    slot_rows = draw_slot_rows(jax.random.fold_in(arg_keys[7], 71), 0)
    slot_cols = draw_slot_cols(jax.random.fold_in(arg_keys[7], 71), 0)
    slot_count = draw_slot_count(jax.random.fold_in(arg_keys[7], 71), 0)
    cell_class = with_ends(jax.random.randint(arg_keys[4], (COL_BLOCKS, STRIDE, BLOCK), 0, CLASSES), jax.random.fold_in(arg_keys[4], 1), 0, CLASSES - 1).astype(jnp.int32)
    class_contrast = jnp.clip(jax.random.uniform(arg_keys[5], (CLASSES, 2), jnp.float32, -0.6, 0.6), -0.6, 0.6)
    background = centred(arg_keys[6], (2, SOURCES, COL_BLOCKS, STRIDE, ENTRIES), 1.0, 6.0, ((3, 32),), jnp.float32)
    return {"green_blocks": green_blocks, "slot_rows": slot_rows, "slot_cols": slot_cols, "slot_count": slot_count, "cell_class": cell_class, "class_contrast": class_contrast, "background": background}


def complex_scale(field_now, contrast_re, contrast_im):
    real_part = field_now[0]
    imag_part = field_now[1]
    scaled = jnp.stack([contrast_re * real_part - contrast_im * imag_part, contrast_re * imag_part + contrast_im * real_part])
    return scaled.astype(jnp.bfloat16)


def combine(products):
    return jnp.stack([products[0, 0] - products[1, 1], products[0, 1] + products[1, 0]])


def reference(green_blocks, slot_rows, slot_cols, slot_count, cell_class, class_contrast, background):
    lookup = class_contrast[cell_class].reshape(BLOCKS, BLOCK, 2)
    contrast_re = jnp.tile(lookup[:, :, 0], (1, 3))
    contrast_im = jnp.tile(lookup[:, :, 1], (1, 3))
    start_field = background.reshape(2, SOURCES, BLOCKS, ENTRIES)
    grid_row = jnp.arange(GRID_ROWS, dtype=jnp.int32)[:, None, None]
    grid_col = jnp.arange(STRIDE, dtype=jnp.int32)[None, :, None]
    block_rows = ((slot_rows // 2) * STRIDE + 2 * grid_row + slot_rows % 2).astype(jnp.int32)
    block_cols = (slot_cols * STRIDE + grid_col).astype(jnp.int32)
    living = (jnp.arange(SLOTS, dtype=jnp.int32)[None, None, :] < slot_count[:, :, None]).astype(jnp.float32)
    devices_all = GRID_ROWS * STRIDE
    tiles_all = green_blocks.reshape(devices_all, SLOTS, 2, ENTRIES, ENTRIES)
    rows_flat = block_rows.reshape(devices_all, SLOTS)
    cols_flat = block_cols.reshape(devices_all, SLOTS)
    live_flat = living.reshape(devices_all, SLOTS)

    def apply_operator(current):
        current_wide = lax.optimization_barrier(current).astype(jnp.float32)

        def visit(running, item):
            tiles, rows_here, cols_here, live_here = item
            tiles_wide = tiles.astype(jnp.float32)
            off_diagonal = (rows_here != cols_here).astype(jnp.float32)
            direct_in = jnp.take(current_wide, cols_here, axis=2)
            mirror_in = jnp.take(current_wide, rows_here, axis=2)
            direct_terms = combine(jnp.einsum('sqoi,pksi->qpkso', tiles_wide, direct_in)) * live_here[None, None, :, None]
            mirror_terms = combine(jnp.einsum('sqoi,pkso->qpksi', tiles_wide, mirror_in)) * (live_here * off_diagonal)[None, None, :, None]
            running = running.at[:, :, rows_here].add(direct_terms)
            running = running.at[:, :, cols_here].add(mirror_terms)
            return running, None

        start = jnp.zeros((2, SOURCES, BLOCKS, ENTRIES), jnp.float32)
        return lax.scan(visit, start, (tiles_all, rows_flat, cols_flat, live_flat))[0]

    field_now = start_field
    for step_index in range(PRODUCTS):
        current = complex_scale(field_now, contrast_re, contrast_im)
        field_now = start_field + apply_operator(current)
    return field_now.reshape(2, SOURCES, COL_BLOCKS, STRIDE, ENTRIES)
```

```python
import functools

import jax
import jax.numpy as jnp
from jax import lax
from jax.experimental import pallas as pl
from jax.experimental.pallas import tpu as pltpu
from jax.sharding import PartitionSpec as P

PRODUCTS = 3
SHARDS = 12
GROUPS = 4
MESH = pl.DeviceIdType.MESH
F32 = jnp.float32
BF16 = jnp.bfloat16
NT = (((1,), (1,)), ((), ()))
NN = (((1,), (0,)), ((), ()))


def pack(field):
    rows = field.reshape(2, GROUPS, 8, 4, 288).transpose(1, 0, 2, 3, 4).reshape(GROUPS, 16, 4, 288)
    main = rows[..., :256].reshape(GROUPS, 16, 1024)
    tail = rows[..., 256:].reshape(GROUPS, 16, 128)
    lanes = jnp.concatenate([main, tail], axis=-1).reshape(GROUPS, 16, 3, 384)
    return lanes.transpose(0, 2, 1, 3).reshape(SHARDS, 16, 384)


def unpack(shards):
    lanes = shards.reshape(GROUPS, 3, 16, 384).transpose(0, 2, 1, 3).reshape(GROUPS, 16, 1152)
    main = lanes[..., :1024].reshape(GROUPS, 16, 4, 256)
    tail = lanes[..., 1024:].reshape(GROUPS, 16, 4, 32)
    rows = jnp.concatenate([main, tail], axis=-1).reshape(GROUPS, 2, 8, 4, 288)
    return rows.transpose(1, 0, 2, 3, 4).reshape(2, 32, 4, 288)


def kernel(
    n_rows,
    rows_ref,
    cols_ref,
    row_pick,
    col_pick,
    g_hbm,
    first_ref,
    back_ref,
    scale_ref,
    out_ref,
    g,
    own,
    across,
    left_own,
    left_across,
    terms,
    half,
    half_in,
    direct,
    mirror,
    arrived,
    now,
    g_sem,
    own_sem,
    across_sem,
    swap_sem,
    half_sem,
    arrived_sem,
    out_sem,
    send_first,
    send_swap,
    send_half,
    send_direct,
    send_mirror,
    send_now,
):
    slots = g.shape[0]
    r = lax.axis_index("row")
    c = lax.axis_index("col")
    s, k = c // 2, c % 2
    shard = (r - s + n_rows) % n_rows
    diagonal = r == s
    reducer = shard < SHARDS
    other = (r, 2 * s + 1 - k)

    loads = pltpu.make_async_copy(g_hbm.at[0, 0], g, g_sem)
    loads.start()

    barrier = pltpu.get_barrier_semaphore()

    def greet(row, col):
        pl.semaphore_signal(barrier, inc=1, device_id=(row, col), device_id_type=MESH)

    greet(*other)

    def greet_all(d, _):
        @pl.when(d > 0)
        def _():
            greet((r + d) % n_rows, c)

        @pl.when(jnp.logical_and(d > 0, (s + d) % n_rows != r))
        def _():
            greet(s, 2 * ((s + d) % n_rows) + k)

        @pl.when(jnp.logical_not(diagonal))
        def _():
            greet((r + d) % n_rows, 2 * r + k)

        return 0

    lax.fori_loop(0, n_rows, greet_all, 0)

    def send(src, dst, send_sem, recv_sem, row, col):
        pltpu.make_async_remote_copy(
            src_ref=src,
            dst_ref=dst,
            send_sem=send_sem,
            recv_sem=recv_sem,
            device_id=(row, col),
            device_id_type=MESH,
        ).start()

    def take(ref, sem):
        pltpu.make_async_copy(ref, ref, sem).wait()

    def unfold(packed, lefts):
        def group(i, _):
            at = pl.ds(pl.multiple_of(16 * i, 16), 16)

            def put(q, lane, value):
                turned = jnp.concatenate([-value[8:], value[:8]], axis=0)
                lefts[q, 0, at, lane : lane + 128] = value.astype(BF16)
                lefts[q, 1, at, lane : lane + 128] = turned.astype(BF16)

            for tile in range(8):
                value = packed[3 * i + tile // 3, :, 128 * (tile % 3) : 128 * (tile % 3) + 128]
                put(tile // 2, 128 * (tile % 2), value.astype(F32))
            tail = packed[3 * i + 2, :, 256:384].astype(F32)
            put(0, 256, tail)
            for q in range(1, 4):
                put(q, 256, pltpu.roll(tail, 128 - 32 * q, 1))
            return 0

        lax.fori_loop(0, GROUPS, group, 0)

    def products(lefts, picks, dims):
        def one(slot, _):
            at = picks[slot]
            re = lefts[at, 0, :, :288]
            im = lefts[at, 1, :, :288]
            terms[slot, :, :288] = lax.dot_general(
                re, g[slot, 0], dims, preferred_element_type=F32
            ) + lax.dot_general(im, g[slot, 1], dims, preferred_element_type=F32)
            return 0

        lax.fori_loop(0, slots, one, 0)

    def gather_terms(pick, first, step, out):
        def group(i, _):
            at = pl.ds(pl.multiple_of(16 * i, 16), 16)
            tail = None
            for q in range(4):
                total = None
                for slot in range(slots):
                    value = terms[slot, at, :] * pick[(first + step * q) * slots + slot]
                    total = value if total is None else total + value
                for part in range(2):
                    tile = 2 * q + part
                    out[3 * i + tile // 3, :, 128 * (tile % 3) : 128 * (tile % 3) + 128] = total[
                        :, 128 * part : 128 * part + 128
                    ].astype(out.dtype)
                last = total[:, 256:384]
                last = pltpu.roll(last, 32 * q, 1) if q else last
                tail = last if tail is None else tail + last
            out[3 * i + 2, :, 256:384] = tail.astype(out.dtype)
            return 0

        lax.fori_loop(0, GROUPS, group, 0)

    terms[:, :, 256:384] = jnp.zeros((slots, 64, 128), F32)
    unfold(first_ref, left_own)

    @pl.when(jnp.logical_not(diagonal))
    def _():
        pl.semaphore_wait(barrier, 3 * n_rows - 2)
        send(first_ref, across.at[0, k], send_first, across_sem.at[0], s, 2 * r + k)

    @pl.when(diagonal)
    def _():
        pl.semaphore_wait(barrier, 2 * n_rows - 1)
        pltpu.make_async_copy(first_ref, across.at[0, k], across_sem.at[0]).start()

    loads.wait()

    def update(step, final):
        products(left_own, cols_ref, NT)
        gather_terms(row_pick, 1 - k, 2, half.at[step, 1])
        send(half.at[step, 1], half_in.at[step], send_half.at[step], half_sem.at[step], *other)
        gather_terms(row_pick, k, 2, half.at[step, 0])

        take(across.at[step, k], across_sem.at[step])
        send(across.at[step, k], across.at[step, k], send_swap.at[step], swap_sem.at[step], *other)

        take(half_in.at[step], half_sem.at[step])

        def send_one(t, _):
            direct[step, t] = (half[step, 0, t] + half_in[step, t]).astype(BF16)
            row = (r + t) % n_rows
            mine = jnp.logical_and(diagonal, t == 0)
            dst = arrived.at[step, s]

            @pl.when(mine)
            def _():
                pltpu.make_async_copy(direct.at[step, t], dst, arrived_sem.at[step]).start()

            @pl.when(jnp.logical_not(mine))
            def _():
                send(direct.at[step, t], dst, send_direct.at[step], arrived_sem.at[step], row, 2 * r + k)

            return 0

        lax.fori_loop(0, SHARDS, send_one, 0)

        unfold(across.at[step, k], left_across.at[k])
        take(across.at[step, 1 - k], swap_sem.at[step])
        unfold(across.at[step, 1 - k], left_across.at[1 - k])
        products_across()
        gather_terms(col_pick, 0, 1, mirror.at[step])

        def send_mine(t, _):
            row = (s + t) % n_rows
            mine = row == r
            dst = arrived.at[step, n_rows + r]

            @pl.when(mine)
            def _():
                pltpu.make_async_copy(mirror.at[step, t], dst, arrived_sem.at[step]).start()

            @pl.when(jnp.logical_not(mine))
            def _():
                send(mirror.at[step, t], dst, send_mirror.at[step], arrived_sem.at[step], row, c)

            return 0

        lax.fori_loop(0, SHARDS, send_mine, 0)

        @pl.when(reducer)
        def _():
            take(arrived.at[step], arrived_sem.at[step])

            def add(j, total):
                return total + arrived[step, j].astype(F32)

            field = lax.fori_loop(0, 2 * n_rows, add, back_ref[shard], unroll=4)
            if final:
                out_ref[shard] = field
            else:
                re, im = field[:8], field[8:]
                scale_re, scale_im = scale_ref[0, shard % 3], scale_ref[1, shard % 3]
                now[step, :8] = (scale_re * re - scale_im * im).astype(BF16)
                now[step, 8:] = (scale_re * im + scale_im * re).astype(BF16)

        if final:
            return

        @pl.when(reducer)
        def _():
            src = now.at[step]
            line = own.at[step, shard]
            plane = across.at[step + 1, k, shard]
            pltpu.make_async_copy(src, line, own_sem.at[step]).start()

            def spread(d, _):
                @pl.when(jnp.logical_or(d > 0, r != s))
                def _():
                    send(src, plane, send_now.at[step], across_sem.at[step + 1], s, 2 * ((s + d) % n_rows) + k)

                @pl.when(jnp.logical_and(d == 0, r == s))
                def _():
                    pltpu.make_async_copy(src, plane, across_sem.at[step + 1]).start()

                @pl.when(d > 0)
                def _():
                    send(src, line, send_now.at[step], own_sem.at[step], (r + d) % n_rows, c)

                return 0

            lax.fori_loop(0, n_rows, spread, 0)

        take(own.at[step], own_sem.at[step])
        unfold(own.at[step], left_own)

    def products_across():
        def one(slot, _):
            at = rows_ref[slot]
            re = left_across[at % 2, at // 2, 0, :, :288]
            im = left_across[at % 2, at // 2, 1, :, :288]
            terms[slot, :, :288] = lax.dot_general(
                re, g[slot, 0], NN, preferred_element_type=F32
            ) + lax.dot_general(im, g[slot, 1], NN, preferred_element_type=F32)
            return 0

        lax.fori_loop(0, slots, one, 0)

    def early(step, _):
        update(step, False)
        return 0

    lax.fori_loop(0, PRODUCTS - 1, early, 0)
    update(PRODUCTS - 1, True)

    @pl.when(reducer)
    def _():
        def spread(d, _):
            send(out_ref.at[shard], out_ref.at[shard], send_now.at[PRODUCTS - 1], out_sem, (r + d) % n_rows, c)
            return 0

        lax.fori_loop(1, n_rows, spread, 0)
        take(out_ref.at[pl.ds(0, SHARDS - 1)], out_sem)
        take(half.at[0, 0], send_now.at[PRODUCTS - 1])
        take(half.at[0, 0, pl.ds(0, n_rows - 1 - SHARDS)], send_now.at[PRODUCTS - 1])

    @pl.when(jnp.logical_not(reducer))
    def _():
        take(out_ref, out_sem)

    @pl.when(jnp.logical_not(diagonal))
    def _():
        take(first_ref, send_first)

    def finish(step, _):
        take(across.at[step, 0], send_swap.at[step])
        take(half_in.at[step], send_half.at[step])

        @pl.when(diagonal)
        def _():
            take(direct.at[step, pl.ds(0, SHARDS - 1)], send_direct.at[step])

        @pl.when(jnp.logical_not(diagonal))
        def _():
            take(direct.at[step], send_direct.at[step])

        @pl.when(reducer)
        def _():
            take(mirror.at[step, pl.ds(0, SHARDS - 1)], send_mirror.at[step])

            @pl.when(step < PRODUCTS - 1)
            def _():
                @pl.when(diagonal)
                def _():
                    take(arrived.at[step, pl.ds(0, 2 * n_rows - 2)], send_now.at[step])

                @pl.when(jnp.logical_not(diagonal))
                def _():
                    take(arrived.at[step, pl.ds(0, 2 * n_rows - 1)], send_now.at[step])

        @pl.when(jnp.logical_not(reducer))
        def _():
            take(mirror.at[step], send_mirror.at[step])

        return 0

    lax.fori_loop(0, PRODUCTS, finish, 0)


def local(n_rows, green_blocks, slot_rows, slot_cols, slot_count, cell_class, class_contrast, background):
    row_index = lax.axis_index("row")
    col_index = lax.axis_index("col")
    stride = lax.axis_size("col")
    slots = green_blocks.shape[2]
    local_rows = slot_rows[0, 0]
    local_cols = slot_cols[0, 0]
    global_rows = local_rows // 2 * stride + 2 * row_index + local_rows % 2
    global_cols = local_cols * stride + col_index
    living = jnp.arange(slots) < slot_count[0, 0]
    row_pick = jnp.where(living & (local_rows == jnp.arange(8)[:, None]), 1.0, 0.0).reshape(-1)
    col_pick = jnp.where(
        living & (global_rows != global_cols) & (local_cols == jnp.arange(4)[:, None]), 1.0, 0.0
    ).reshape(-1)

    classes = class_contrast.shape[0]
    at = cell_class[:, 0, None, :] == jnp.arange(classes)[None, :, None]
    scale = jnp.stack(
        [jnp.sum(jnp.where(at, class_contrast[None, :, part, None], 0.0), axis=1) for part in range(2)]
    )
    scale = jnp.tile(scale, (1, 1, 3))
    lanes = jnp.concatenate(
        [scale[..., :256].reshape(2, 1024), scale[..., 256:].reshape(2, 128)], axis=-1
    ).reshape(2, 3, 1, 384)
    scale = jnp.broadcast_to(lanes, (2, 3, 8, 384))

    back = pack(background[:, :, :, 0, :])
    pairs = back.reshape(GROUPS, 3, 2, 8, 384)
    re, im = pairs[:, :, 0], pairs[:, :, 1]
    first = (
        jnp.stack([scale[0] * re - scale[1] * im, scale[0] * im + scale[1] * re], axis=2)
        .astype(BF16)
        .reshape(SHARDS, 16, 384)
    )

    vmem = pl.BlockSpec(memory_space=pltpu.VMEM)
    smem = pl.BlockSpec(memory_space=pltpu.SMEM)
    packed = (SHARDS, 16, 384)
    steps = (PRODUCTS,)
    dma = pltpu.SemaphoreType.DMA
    field = pl.pallas_call(
        functools.partial(kernel, n_rows),
        out_shape=jax.ShapeDtypeStruct(packed, F32),
        in_specs=[smem] * 4 + [pl.BlockSpec(memory_space=pl.ANY)] + [vmem] * 3,
        out_specs=vmem,
        scratch_shapes=[
            pltpu.VMEM(green_blocks.shape[2:], BF16),
            pltpu.VMEM((PRODUCTS - 1,) + packed, BF16),
            pltpu.VMEM((PRODUCTS, 2) + packed, BF16),
            pltpu.VMEM((4, 2, 64, 384), BF16),
            pltpu.VMEM((2, 4, 2, 64, 384), BF16),
            pltpu.VMEM((slots, 64, 384), F32),
            pltpu.VMEM((PRODUCTS, 2) + packed, F32),
            pltpu.VMEM(steps + packed, F32),
            pltpu.VMEM(steps + packed, BF16),
            pltpu.VMEM(steps + packed, BF16),
            pltpu.VMEM((PRODUCTS, 2 * n_rows, 16, 384), BF16),
            pltpu.VMEM((PRODUCTS, 16, 384), BF16),
            dma(()),
            dma((PRODUCTS - 1,)),
            dma(steps),
            dma(steps),
            dma(steps),
            dma(steps),
            dma(()),
            dma(()),
            dma(steps),
            dma(steps),
            dma(steps),
            dma(steps),
            dma(steps),
        ],
        compiler_params=pltpu.CompilerParams(
            collective_id=0, has_side_effects=True, vmem_limit_bytes=48 * 2**20
        ),
    )(local_rows, local_cols, row_pick, col_pick, green_blocks, first, back, scale)
    return unpack(field)[:, :, :, None, :]


def solution(mesh):
    in_specs = (
        P("row", "col", None, None, None, None),
        P("row", "col", None),
        P("row", "col", None),
        P("row", "col"),
        P(None, "col", None),
        P(),
        P(None, None, None, "col", None),
    )
    out_specs = P(None, None, None, "col", None)
    return jax.shard_map(
        functools.partial(local, mesh.shape["row"]),
        mesh=mesh,
        in_specs=in_specs,
        out_specs=out_specs,
        check_vma=False,
    )
```

```python
import functools

import jax
import jax.numpy as jnp
from jax import lax
from jax.experimental import pallas as pl
from jax.experimental.pallas import tpu as pltpu
from jax.sharding import PartitionSpec as P

PRODUCTS = 3
SHARDS = 12
TURN = 4
GROUPS = 4
MESH = pl.DeviceIdType.MESH
F32 = jnp.float32
BF16 = jnp.bfloat16
NT = (((1,), (1,)), ((), ()))
NN = (((1,), (0,)), ((), ()))


def pack(field):
    rows = field.reshape(2, GROUPS, 8, 4, 288).transpose(1, 0, 2, 3, 4).reshape(GROUPS, 16, 4, 288)
    main = rows[..., :256].reshape(GROUPS, 16, 1024)
    tail = rows[..., 256:].reshape(GROUPS, 16, 128)
    lanes = jnp.concatenate([main, tail], axis=-1).reshape(GROUPS, 16, 3, 384)
    return lanes.transpose(0, 2, 1, 3).reshape(SHARDS, 16, 384)


def unpack(shards):
    lanes = shards.reshape(GROUPS, 3, 16, 384).transpose(0, 2, 1, 3).reshape(GROUPS, 16, 1152)
    main = lanes[..., :1024].reshape(GROUPS, 16, 4, 256)
    tail = lanes[..., 1024:].reshape(GROUPS, 16, 4, 32)
    rows = jnp.concatenate([main, tail], axis=-1).reshape(GROUPS, 2, 8, 4, 288)
    return rows.transpose(1, 0, 2, 3, 4).reshape(2, 32, 4, 288)


def kernel(
    n_rows,
    rows_ref,
    cols_ref,
    row_pick,
    col_pick,
    g_hbm,
    first_ref,
    back_ref,
    scale_ref,
    out_ref,
    g,
    own,
    across,
    left_own,
    left_across,
    terms,
    half,
    half_in,
    direct,
    mirror,
    arrived,
    now,
    last,
    give,
    given,
    g_sem,
    own_sem,
    across_sem,
    swap_sem,
    half_sem,
    arrived_sem,
    out_sem,
    send_first,
    send_swap,
    send_half,
    send_direct,
    send_mirror,
    send_now,
    given_sem,
    send_given,
):
    slots = g.shape[0]
    r = lax.axis_index("row")
    c = lax.axis_index("col")
    s, k = c // 2, c % 2
    side = n_rows // 4
    diagonal = r == s
    other = (r, 2 * s + 1 - k)

    def turn(row):
        return (row // 2) % TURN

    def place(t):
        return 4 * (t // 3) + t % 3 + (t % 3) // 2 * (t // 3 % 2)

    def seat(h, row):
        return (h // side + turn(row)) % 4 * side + h % side

    hub = (s // side + 4 - turn(r)) % 4 * side + s % side
    reducer = jnp.logical_or(r % 4 < 2, r % 4 == 2 + r // 4 % 2)
    shard = 3 * (r // 4) + jnp.minimum(r % 4, 2)
    in_line = jnp.logical_and(reducer, hub == s)
    in_plane = jnp.logical_and(reducer, hub == r)

    loads = pltpu.make_async_copy(g_hbm.at[0, 0], g, g_sem)
    loads.start()

    barrier = pltpu.get_barrier_semaphore()

    def greet(row, col):
        pl.semaphore_signal(barrier, inc=1, device_id=(row, col), device_id_type=MESH)

    greet(*other)

    def greet_reducers(t, _):
        row = place(t)

        @pl.when(jnp.logical_not(jnp.logical_and(row == r, in_line)))
        def _():
            greet(row, 2 * seat(s, row) + k)

        @pl.when(jnp.logical_not(jnp.logical_and(row == r, in_plane)))
        def _():
            greet(row, 2 * seat(r, row) + k)

        return 0

    lax.fori_loop(0, SHARDS, greet_reducers, 0)

    @pl.when(reducer)
    def _():
        def greet_members(d, _):
            @pl.when(jnp.logical_not(jnp.logical_and(d == r, in_line)))
            def _():
                greet(d, 2 * hub + k)

            @pl.when(jnp.logical_not(jnp.logical_and(d == s, in_plane)))
            def _():
                greet(hub, 2 * d + k)

            return 0

        lax.fori_loop(0, n_rows, greet_members, 0)

    @pl.when(jnp.logical_not(diagonal))
    def _():
        greet(s, 2 * r + k)

    greeted = (
        1
        + jnp.where(diagonal, 0, 1)
        + 2 * SHARDS
        + jnp.where(reducer, 2 * n_rows, 0)
        - jnp.where(in_line, 2, 0)
        - jnp.where(in_plane, 2, 0)
    )

    def send(src, dst, send_sem, recv_sem, row, col):
        pltpu.make_async_remote_copy(
            src_ref=src,
            dst_ref=dst,
            send_sem=send_sem,
            recv_sem=recv_sem,
            device_id=(row, col),
            device_id_type=MESH,
        ).start()

    def take(ref, sem):
        pltpu.make_async_copy(ref, ref, sem).wait()

    def spread(src, dst, send_sem, recv_sem, d):
        mine = jnp.logical_and(d == r, in_line)

        @pl.when(mine)
        def _():
            pltpu.make_async_copy(src, dst, recv_sem).start()

        @pl.when(jnp.logical_not(mine))
        def _():
            send(src, dst, send_sem, recv_sem, d, 2 * hub + k)

    def unfold(packed, lefts):
        def group(i, _):
            at = pl.ds(pl.multiple_of(16 * i, 16), 16)

            def put(q, lane, value):
                turned = jnp.concatenate([-value[8:], value[:8]], axis=0)
                lefts[q, 0, at, lane : lane + 128] = value.astype(BF16)
                lefts[q, 1, at, lane : lane + 128] = turned.astype(BF16)

            for tile in range(8):
                value = packed[3 * i + tile // 3, :, 128 * (tile % 3) : 128 * (tile % 3) + 128]
                put(tile // 2, 128 * (tile % 2), value.astype(F32))
            tail = packed[3 * i + 2, :, 256:384].astype(F32)
            put(0, 256, tail)
            for q in range(1, 4):
                put(q, 256, pltpu.roll(tail, 128 - 32 * q, 1))
            return 0

        lax.fori_loop(0, GROUPS, group, 0)

    def products(lefts, picks, dims):
        def one(slot, _):
            at = picks[slot]
            re = lefts[at, 0, :, :288]
            im = lefts[at, 1, :, :288]
            terms[slot, :, :288] = lax.dot_general(
                re, g[slot, 0], dims, preferred_element_type=F32
            ) + lax.dot_general(im, g[slot, 1], dims, preferred_element_type=F32)
            return 0

        lax.fori_loop(0, slots, one, 0)

    def gather_terms(pick, first, step, out):
        def group(i, _):
            at = pl.ds(pl.multiple_of(16 * i, 16), 16)
            tail = None
            for q in range(4):
                total = None
                for slot in range(slots):
                    value = terms[slot, at, :] * pick[(first + step * q) * slots + slot]
                    total = value if total is None else total + value
                for part in range(2):
                    tile = 2 * q + part
                    out[3 * i + tile // 3, :, 128 * (tile % 3) : 128 * (tile % 3) + 128] = total[
                        :, 128 * part : 128 * part + 128
                    ].astype(out.dtype)
                last = total[:, 256:384]
                last = pltpu.roll(last, 32 * q, 1) if q else last
                tail = last if tail is None else tail + last
            out[3 * i + 2, :, 256:384] = tail.astype(out.dtype)
            return 0

        lax.fori_loop(0, GROUPS, group, 0)

    terms[:, :, 256:384] = jnp.zeros((slots, 64, 128), F32)
    unfold(first_ref, left_own)

    pl.semaphore_wait(barrier, greeted)

    @pl.when(jnp.logical_not(diagonal))
    def _():
        send(first_ref, across.at[0, k], send_first, across_sem.at[0], s, 2 * r + k)

    @pl.when(diagonal)
    def _():
        pltpu.make_async_copy(first_ref, across.at[0, k], across_sem.at[0]).start()

    @pl.when(reducer)
    def _():
        give[0] = back_ref[shard]
        give[1] = scale_ref[shard % 3]

        @pl.when(in_line)
        def _():
            pltpu.make_async_copy(give, given, given_sem).start()

        @pl.when(jnp.logical_not(in_line))
        def _():
            send(give, given, send_given, given_sem, r, 2 * seat(s, r) + k)

    loads.wait()

    def update(step, final):
        products(left_own, cols_ref, NT)
        gather_terms(row_pick, 1 - k, 2, half.at[step, 1])
        send(half.at[step, 1], half_in.at[step], send_half.at[step], half_sem.at[step], *other)
        gather_terms(row_pick, k, 2, half.at[step, 0])

        take(half_in.at[step], half_sem.at[step])

        def send_one(t, _):
            direct[step, t] = (half[step, 0, t] + half_in[step, t]).astype(BF16)
            row = place(t)
            mine = jnp.logical_and(row == r, in_plane)
            dst = arrived.at[step, s]

            @pl.when(mine)
            def _():
                pltpu.make_async_copy(direct.at[step, t], dst, arrived_sem.at[step]).start()

            @pl.when(jnp.logical_not(mine))
            def _():
                send(direct.at[step, t], dst, send_direct.at[step], arrived_sem.at[step], row, 2 * seat(r, row) + k)

            return 0

        lax.fori_loop(0, SHARDS, send_one, 0)

        take(across.at[step, k], across_sem.at[step])
        send(across.at[step, k], across.at[step, k], send_swap.at[step], swap_sem.at[step], *other)
        unfold(across.at[step, k], left_across.at[k])
        take(across.at[step, 1 - k], swap_sem.at[step])
        unfold(across.at[step, 1 - k], left_across.at[1 - k])
        products_across()
        gather_terms(col_pick, 0, 1, mirror.at[step])

        def send_mine(t, _):
            row = place(t)
            mine = jnp.logical_and(row == r, in_line)
            dst = arrived.at[step, n_rows + r]

            @pl.when(mine)
            def _():
                pltpu.make_async_copy(mirror.at[step, t], dst, arrived_sem.at[step]).start()

            @pl.when(jnp.logical_not(mine))
            def _():
                send(mirror.at[step, t], dst, send_mirror.at[step], arrived_sem.at[step], row, 2 * seat(s, row) + k)

            return 0

        lax.fori_loop(0, SHARDS, send_mine, 0)

        @pl.when(reducer)
        def _():
            take(arrived.at[step], arrived_sem.at[step])

            def add(j, total):
                return total + arrived[step, j].astype(F32)


            @pl.when(step == 0)
            def _():
                take(given, given_sem)

            field = lax.fori_loop(0, 2 * n_rows, add, given[0], unroll=4)
            if final:
                last[...] = field
            else:
                re, im = field[:8], field[8:]
                scale_re, scale_im = given[1, :8], given[1, 8:]
                now[step, :8] = (scale_re * re - scale_im * im).astype(BF16)
                now[step, 8:] = (scale_re * im + scale_im * re).astype(BF16)

        if final:
            return

        @pl.when(reducer)
        def _():
            src = now.at[step]
            line = own.at[step, shard]
            plane = across.at[step + 1, k, shard]

            def spread_line(d, _):
                spread(src, line, send_now.at[step], own_sem.at[step], d)
                return 0

            lax.fori_loop(0, n_rows, spread_line, 0)

            def spread_plane(d, _):
                mine = jnp.logical_and(d == s, in_plane)

                @pl.when(mine)
                def _():
                    pltpu.make_async_copy(src, plane, across_sem.at[step + 1]).start()

                @pl.when(jnp.logical_not(mine))
                def _():
                    send(src, plane, send_now.at[step], across_sem.at[step + 1], hub, 2 * d + k)

                return 0

            lax.fori_loop(0, n_rows, spread_plane, 0)

        take(own.at[step], own_sem.at[step])
        unfold(own.at[step], left_own)

    def products_across():
        def one(slot, _):
            at = rows_ref[slot]
            re = left_across[at % 2, at // 2, 0, :, :288]
            im = left_across[at % 2, at // 2, 1, :, :288]
            terms[slot, :, :288] = lax.dot_general(
                re, g[slot, 0], NN, preferred_element_type=F32
            ) + lax.dot_general(im, g[slot, 1], NN, preferred_element_type=F32)
            return 0

        lax.fori_loop(0, slots, one, 0)

    def early(step, _):
        update(step, False)
        return 0

    lax.fori_loop(0, PRODUCTS - 1, early, 0)
    update(PRODUCTS - 1, True)

    @pl.when(reducer)
    def _():
        def spread_last(d, _):
            spread(last, out_ref.at[shard], send_now.at[PRODUCTS - 1], out_sem, d)
            return 0

        lax.fori_loop(0, n_rows, spread_last, 0)

    take(out_ref, out_sem)

    @pl.when(in_line)
    def _():
        take(arrived.at[0, pl.ds(0, 2 * n_rows - 2)], send_now.at[PRODUCTS - 1])

    @pl.when(jnp.logical_and(reducer, hub != s))
    def _():
        take(arrived.at[0], send_now.at[PRODUCTS - 1])
        take(given, send_given)

    @pl.when(jnp.logical_not(diagonal))
    def _():
        take(first_ref, send_first)

    def finish(step, _):
        take(across.at[step, 0], send_swap.at[step])
        take(half_in.at[step], send_half.at[step])

        def sent(ref, less, send_sem):
            @pl.when(less)
            def _():
                take(ref.at[pl.ds(0, SHARDS - 1)], send_sem)

            @pl.when(jnp.logical_not(less))
            def _():
                take(ref, send_sem)

        sent(direct.at[step], in_plane, send_direct.at[step])
        sent(mirror.at[step], in_line, send_mirror.at[step])

        @pl.when(jnp.logical_and(reducer, step < PRODUCTS - 1))
        def _():
            both = jnp.logical_and(in_line, in_plane)
            either = jnp.logical_or(in_line, in_plane)

            @pl.when(both)
            def _():
                take(arrived.at[step, pl.ds(0, 2 * n_rows - 2)], send_now.at[step])

            @pl.when(jnp.logical_and(either, jnp.logical_not(both)))
            def _():
                take(arrived.at[step, pl.ds(0, 2 * n_rows - 1)], send_now.at[step])

            @pl.when(jnp.logical_not(either))
            def _():
                take(arrived.at[step], send_now.at[step])

        return 0

    lax.fori_loop(0, PRODUCTS, finish, 0)


def local(n_rows, green_blocks, slot_rows, slot_cols, slot_count, cell_class, class_contrast, background):
    row_index = lax.axis_index("row")
    col_index = lax.axis_index("col")
    stride = lax.axis_size("col")
    slots = green_blocks.shape[2]
    local_rows = slot_rows[0, 0]
    local_cols = slot_cols[0, 0]
    global_rows = local_rows // 2 * stride + 2 * row_index + local_rows % 2
    global_cols = local_cols * stride + col_index
    living = jnp.arange(slots) < slot_count[0, 0]
    row_pick = jnp.where(living & (local_rows == jnp.arange(8)[:, None]), 1.0, 0.0).reshape(-1)
    col_pick = jnp.where(
        living & (global_rows != global_cols) & (local_cols == jnp.arange(4)[:, None]), 1.0, 0.0
    ).reshape(-1)

    classes = class_contrast.shape[0]
    at = cell_class[:, 0, None, :] == jnp.arange(classes)[None, :, None]
    scale = jnp.stack(
        [jnp.sum(jnp.where(at, class_contrast[None, :, part, None], 0.0), axis=1) for part in range(2)]
    )
    scale = jnp.tile(scale, (1, 1, 3))
    lanes = jnp.concatenate(
        [scale[..., :256].reshape(2, 1024), scale[..., 256:].reshape(2, 128)], axis=-1
    ).reshape(2, 3, 384)
    scale = jnp.broadcast_to(lanes.transpose(1, 0, 2)[:, :, None], (3, 2, 8, 384)).reshape(3, 16, 384)
    scale_re, scale_im = lanes[0, :, None], lanes[1, :, None]

    back = pack(background[:, :, :, 0, :])
    pairs = back.reshape(GROUPS, 3, 2, 8, 384)
    re, im = pairs[:, :, 0], pairs[:, :, 1]
    first = (
        jnp.stack([scale_re * re - scale_im * im, scale_re * im + scale_im * re], axis=2)
        .astype(BF16)
        .reshape(SHARDS, 16, 384)
    )

    vmem = pl.BlockSpec(memory_space=pltpu.VMEM)
    smem = pl.BlockSpec(memory_space=pltpu.SMEM)
    packed = (SHARDS, 16, 384)
    steps = (PRODUCTS,)
    dma = pltpu.SemaphoreType.DMA
    field = pl.pallas_call(
        functools.partial(kernel, n_rows),
        out_shape=jax.ShapeDtypeStruct(packed, F32),
        in_specs=[smem] * 4 + [pl.BlockSpec(memory_space=pltpu.HBM)] + [vmem] * 3,
        out_specs=vmem,
        scratch_shapes=[
            pltpu.VMEM(green_blocks.shape[2:], BF16),
            pltpu.VMEM((PRODUCTS - 1,) + packed, BF16),
            pltpu.VMEM((PRODUCTS, 2) + packed, BF16),
            pltpu.VMEM((4, 2, 64, 384), BF16),
            pltpu.VMEM((2, 4, 2, 64, 384), BF16),
            pltpu.VMEM((slots, 64, 384), F32),
            pltpu.VMEM((PRODUCTS, 2) + packed, F32),
            pltpu.VMEM(steps + packed, F32),
            pltpu.VMEM(steps + packed, BF16),
            pltpu.VMEM(steps + packed, BF16),
            pltpu.VMEM((PRODUCTS, 2 * n_rows, 16, 384), BF16),
            pltpu.VMEM((PRODUCTS, 16, 384), BF16),
            pltpu.VMEM((16, 384), F32),
            pltpu.VMEM((2, 16, 384), F32),
            pltpu.VMEM((2, 16, 384), F32),
            dma(()),
            dma((PRODUCTS - 1,)),
            dma(steps),
            dma(steps),
            dma(steps),
            dma(steps),
            dma(()),
            dma(()),
            dma(steps),
            dma(steps),
            dma(steps),
            dma(steps),
            dma(steps),
            dma(()),
            dma(()),
        ],
        compiler_params=pltpu.CompilerParams(
            collective_id=0, has_side_effects=True, vmem_limit_bytes=60 * 2**20
        ),
    )(local_rows, local_cols, row_pick, col_pick, green_blocks, first, back, scale)
    return unpack(field)[:, :, :, None, :]


def solution(mesh):
    in_specs = (
        P("row", "col", None, None, None, None),
        P("row", "col", None),
        P("row", "col", None),
        P("row", "col"),
        P(None, "col", None),
        P(),
        P(None, None, None, "col", None),
    )
    out_specs = P(None, None, None, "col", None)
    return jax.shard_map(
        functools.partial(local, mesh.shape["row"]),
        mesh=mesh,
        in_specs=in_specs,
        out_specs=out_specs,
        check_vma=False,
    )
```

```python
import functools

import jax
import jax.numpy as jnp
from jax import lax
from jax.experimental import pallas as pl
from jax.experimental.pallas import tpu as pltpu
from jax.sharding import PartitionSpec as P

PRODUCTS = 3
SHARDS = 12
TURN = 4
GROUPS = 4
MESH = pl.DeviceIdType.MESH
F32 = jnp.float32
BF16 = jnp.bfloat16
NT = (((1,), (1,)), ((), ()))
NN = (((1,), (0,)), ((), ()))


def pack(field):
    rows = field.reshape(2, GROUPS, 8, 4, 288).transpose(1, 0, 2, 3, 4).reshape(GROUPS, 16, 4, 288)
    main = rows[..., :256].reshape(GROUPS, 16, 1024)
    tail = rows[..., 256:].reshape(GROUPS, 16, 128)
    lanes = jnp.concatenate([main, tail], axis=-1).reshape(GROUPS, 16, 3, 384)
    return lanes.transpose(0, 2, 1, 3).reshape(SHARDS, 16, 384)


def unpack(shards):
    lanes = shards.reshape(GROUPS, 3, 16, 384).transpose(0, 2, 1, 3).reshape(GROUPS, 16, 1152)
    main = lanes[..., :1024].reshape(GROUPS, 16, 4, 256)
    tail = lanes[..., 1024:].reshape(GROUPS, 16, 4, 32)
    rows = jnp.concatenate([main, tail], axis=-1).reshape(GROUPS, 2, 8, 4, 288)
    return rows.transpose(1, 0, 2, 3, 4).reshape(2, 32, 4, 288)


def kernel(
    n_rows,
    rows_ref,
    cols_ref,
    row_pick,
    col_pick,
    g_hbm,
    first_ref,
    back_ref,
    scale_ref,
    out_ref,
    g,
    own,
    across,
    left_own,
    left_across,
    terms,
    half,
    half_in,
    direct,
    mirror,
    arrived,
    now,
    last,
    give,
    given,
    g_sem,
    own_sem,
    across_sem,
    swap_sem,
    half_sem,
    arrived_sem,
    out_sem,
    send_first,
    send_swap,
    send_half,
    send_direct,
    send_mirror,
    send_now,
    given_sem,
    send_given,
):
    slots = g.shape[0]
    r = lax.axis_index("row")
    c = lax.axis_index("col")
    s, k = c // 2, c % 2
    side = n_rows // 4
    diagonal = r == s
    other = (r, 2 * s + 1 - k)

    def turn(row):
        return (row // 2) % TURN

    def place(t):
        return 4 * (t // 3) + t % 3 + (t % 3) // 2 * (t // 3 % 2)

    def seat(h, row):
        return (h // side + turn(row)) % 4 * side + h % side

    hub = (s // side + 4 - turn(r)) % 4 * side + s % side
    reducer = jnp.logical_or(r % 4 < 2, r % 4 == 2 + r // 4 % 2)
    shard = 3 * (r // 4) + jnp.minimum(r % 4, 2)
    in_line = jnp.logical_and(reducer, hub == s)
    in_plane = jnp.logical_and(reducer, hub == r)

    loads = pltpu.make_async_copy(g_hbm.at[0, 0], g, g_sem)
    loads.start()

    barrier = pltpu.get_barrier_semaphore()

    def greet(row, col):
        pl.semaphore_signal(barrier, inc=1, device_id=(row, col), device_id_type=MESH)

    greet(*other)

    def greet_reducers(t, _):
        row = place(t)

        @pl.when(jnp.logical_not(jnp.logical_and(row == r, in_line)))
        def _():
            greet(row, 2 * seat(s, row) + k)

        @pl.when(jnp.logical_not(jnp.logical_and(row == r, in_plane)))
        def _():
            greet(row, 2 * seat(r, row) + k)

        return 0

    lax.fori_loop(0, SHARDS, greet_reducers, 0)

    @pl.when(reducer)
    def _():
        def greet_members(d, _):
            @pl.when(jnp.logical_not(jnp.logical_and(d == r, in_line)))
            def _():
                greet(d, 2 * hub + k)

            @pl.when(jnp.logical_not(jnp.logical_and(d == s, in_plane)))
            def _():
                greet(hub, 2 * d + k)

            return 0

        lax.fori_loop(0, n_rows, greet_members, 0)

    @pl.when(jnp.logical_not(diagonal))
    def _():
        greet(s, 2 * r + k)

    greeted = (
        1
        + jnp.where(diagonal, 0, 1)
        + 2 * SHARDS
        + jnp.where(reducer, 2 * n_rows, 0)
        - jnp.where(in_line, 2, 0)
        - jnp.where(in_plane, 2, 0)
    )

    def send(src, dst, send_sem, recv_sem, row, col):
        pltpu.make_async_remote_copy(
            src_ref=src,
            dst_ref=dst,
            send_sem=send_sem,
            recv_sem=recv_sem,
            device_id=(row, col),
            device_id_type=MESH,
        ).start()

    def take(ref, sem):
        pltpu.make_async_copy(ref, ref, sem).wait()

    def spread(src, dst, send_sem, recv_sem, d):
        mine = jnp.logical_and(d == r, in_line)

        @pl.when(mine)
        def _():
            pltpu.make_async_copy(src, dst, recv_sem).start()

        @pl.when(jnp.logical_not(mine))
        def _():
            send(src, dst, send_sem, recv_sem, d, 2 * hub + k)

    def unfold(packed, lefts):
        def group(i, _):
            at = pl.ds(pl.multiple_of(16 * i, 16), 16)

            def put(q, lane, value):
                turned = jnp.concatenate([-value[8:], value[:8]], axis=0)
                lefts[q, 0, at, lane : lane + 128] = value.astype(BF16)
                lefts[q, 1, at, lane : lane + 128] = turned.astype(BF16)

            for tile in range(8):
                value = packed[3 * i + tile // 3, :, 128 * (tile % 3) : 128 * (tile % 3) + 128]
                put(tile // 2, 128 * (tile % 2), value.astype(F32))
            tail = packed[3 * i + 2, :, 256:384].astype(F32)
            put(0, 256, tail)
            for q in range(1, 4):
                put(q, 256, pltpu.roll(tail, 128 - 32 * q, 1))
            return 0

        lax.fori_loop(0, GROUPS, group, 0, unroll=True)

    def products(lefts, picks, dims):
        def one(slot, _):
            at = picks[slot]
            re = lefts[at, 0, :, :288]
            im = lefts[at, 1, :, :288]
            terms[slot, :, :288] = lax.dot_general(
                re, g[slot, 0], dims, preferred_element_type=F32
            ) + lax.dot_general(im, g[slot, 1], dims, preferred_element_type=F32)
            return 0

        lax.fori_loop(0, slots, one, 0, unroll=4)

    def gather_terms(pick, first, step, out):
        def group(i, _):
            at = pl.ds(pl.multiple_of(16 * i, 16), 16)
            tail = None
            for q in range(4):
                total = None
                for slot in range(slots):
                    value = terms[slot, at, :] * pick[(first + step * q) * slots + slot]
                    total = value if total is None else total + value
                for part in range(2):
                    tile = 2 * q + part
                    out[3 * i + tile // 3, :, 128 * (tile % 3) : 128 * (tile % 3) + 128] = total[
                        :, 128 * part : 128 * part + 128
                    ].astype(out.dtype)
                last = total[:, 256:384]
                last = pltpu.roll(last, 32 * q, 1) if q else last
                tail = last if tail is None else tail + last
            out[3 * i + 2, :, 256:384] = tail.astype(out.dtype)
            return 0

        lax.fori_loop(0, GROUPS, group, 0, unroll=True)

    terms[:, :, 256:384] = jnp.zeros((slots, 64, 128), F32)
    unfold(first_ref, left_own)

    pl.semaphore_wait(barrier, greeted)

    @pl.when(jnp.logical_not(diagonal))
    def _():
        send(first_ref, across.at[0, k], send_first, across_sem.at[0], s, 2 * r + k)

    @pl.when(diagonal)
    def _():
        pltpu.make_async_copy(first_ref, across.at[0, k], across_sem.at[0]).start()

    @pl.when(reducer)
    def _():
        give[0] = back_ref[shard]
        give[1] = scale_ref[shard % 3]

        @pl.when(in_line)
        def _():
            pltpu.make_async_copy(give, given, given_sem).start()

        @pl.when(jnp.logical_not(in_line))
        def _():
            send(give, given, send_given, given_sem, r, 2 * seat(s, r) + k)

    loads.wait()

    def update(step, final):
        products(left_own, cols_ref, NT)
        gather_terms(row_pick, 1 - k, 2, half.at[step, 1])
        send(half.at[step, 1], half_in.at[step], send_half.at[step], half_sem.at[step], *other)
        gather_terms(row_pick, k, 2, half.at[step, 0])

        take(half_in.at[step], half_sem.at[step])

        def send_one(t, _):
            direct[step, t] = (half[step, 0, t] + half_in[step, t]).astype(BF16)
            row = place(t)
            mine = jnp.logical_and(row == r, in_plane)
            dst = arrived.at[step, s]

            @pl.when(mine)
            def _():
                pltpu.make_async_copy(direct.at[step, t], dst, arrived_sem.at[step]).start()

            @pl.when(jnp.logical_not(mine))
            def _():
                send(direct.at[step, t], dst, send_direct.at[step], arrived_sem.at[step], row, 2 * seat(r, row) + k)

            return 0

        lax.fori_loop(0, SHARDS, send_one, 0)

        take(across.at[step, k], across_sem.at[step])
        send(across.at[step, k], across.at[step, k], send_swap.at[step], swap_sem.at[step], *other)
        unfold(across.at[step, k], left_across.at[k])
        take(across.at[step, 1 - k], swap_sem.at[step])
        unfold(across.at[step, 1 - k], left_across.at[1 - k])
        products_across()
        gather_terms(col_pick, 0, 1, mirror.at[step])

        def send_mine(t, _):
            row = place(t)
            mine = jnp.logical_and(row == r, in_line)
            dst = arrived.at[step, n_rows + r]

            @pl.when(mine)
            def _():
                pltpu.make_async_copy(mirror.at[step, t], dst, arrived_sem.at[step]).start()

            @pl.when(jnp.logical_not(mine))
            def _():
                send(mirror.at[step, t], dst, send_mirror.at[step], arrived_sem.at[step], row, 2 * seat(s, row) + k)

            return 0

        lax.fori_loop(0, SHARDS, send_mine, 0)

        @pl.when(reducer)
        def _():
            take(arrived.at[step], arrived_sem.at[step])

            def add(j, total):
                return total + arrived[step, j].astype(F32)


            @pl.when(step == 0)
            def _():
                take(given, given_sem)

            field = lax.fori_loop(0, 2 * n_rows, add, given[0], unroll=8)
            if final:
                last[...] = field
            else:
                re, im = field[:8], field[8:]
                scale_re, scale_im = given[1, :8], given[1, 8:]
                now[step, :8] = (scale_re * re - scale_im * im).astype(BF16)
                now[step, 8:] = (scale_re * im + scale_im * re).astype(BF16)

        if final:
            return

        @pl.when(reducer)
        def _():
            src = now.at[step]
            line = own.at[step, shard]
            plane = across.at[step + 1, k, shard]

            def spread_line(d, _):
                spread(src, line, send_now.at[step], own_sem.at[step], d)
                return 0

            lax.fori_loop(0, n_rows, spread_line, 0)

            def spread_plane(d, _):
                mine = jnp.logical_and(d == s, in_plane)

                @pl.when(mine)
                def _():
                    pltpu.make_async_copy(src, plane, across_sem.at[step + 1]).start()

                @pl.when(jnp.logical_not(mine))
                def _():
                    send(src, plane, send_now.at[step], across_sem.at[step + 1], hub, 2 * d + k)

                return 0

            lax.fori_loop(0, n_rows, spread_plane, 0)

        take(own.at[step], own_sem.at[step])
        unfold(own.at[step], left_own)

    def products_across():
        def one(slot, _):
            at = rows_ref[slot]
            re = left_across[at % 2, at // 2, 0, :, :288]
            im = left_across[at % 2, at // 2, 1, :, :288]
            terms[slot, :, :288] = lax.dot_general(
                re, g[slot, 0], NN, preferred_element_type=F32
            ) + lax.dot_general(im, g[slot, 1], NN, preferred_element_type=F32)
            return 0

        lax.fori_loop(0, slots, one, 0, unroll=4)

    def early(step, _):
        update(step, False)
        return 0

    lax.fori_loop(0, PRODUCTS - 1, early, 0)
    update(PRODUCTS - 1, True)

    @pl.when(reducer)
    def _():
        def spread_last(d, _):
            spread(last, out_ref.at[shard], send_now.at[PRODUCTS - 1], out_sem, d)
            return 0

        lax.fori_loop(0, n_rows, spread_last, 0)

    take(out_ref, out_sem)

    @pl.when(in_line)
    def _():
        take(arrived.at[0, pl.ds(0, 2 * n_rows - 2)], send_now.at[PRODUCTS - 1])

    @pl.when(jnp.logical_and(reducer, hub != s))
    def _():
        take(arrived.at[0], send_now.at[PRODUCTS - 1])
        take(given, send_given)

    @pl.when(jnp.logical_not(diagonal))
    def _():
        take(first_ref, send_first)

    def finish(step, _):
        take(across.at[step, 0], send_swap.at[step])
        take(half_in.at[step], send_half.at[step])

        def sent(ref, less, send_sem):
            @pl.when(less)
            def _():
                take(ref.at[pl.ds(0, SHARDS - 1)], send_sem)

            @pl.when(jnp.logical_not(less))
            def _():
                take(ref, send_sem)

        sent(direct.at[step], in_plane, send_direct.at[step])
        sent(mirror.at[step], in_line, send_mirror.at[step])

        @pl.when(jnp.logical_and(reducer, step < PRODUCTS - 1))
        def _():
            both = jnp.logical_and(in_line, in_plane)
            either = jnp.logical_or(in_line, in_plane)

            @pl.when(both)
            def _():
                take(arrived.at[step, pl.ds(0, 2 * n_rows - 2)], send_now.at[step])

            @pl.when(jnp.logical_and(either, jnp.logical_not(both)))
            def _():
                take(arrived.at[step, pl.ds(0, 2 * n_rows - 1)], send_now.at[step])

            @pl.when(jnp.logical_not(either))
            def _():
                take(arrived.at[step], send_now.at[step])

        return 0

    lax.fori_loop(0, PRODUCTS, finish, 0)


def local(n_rows, green_blocks, slot_rows, slot_cols, slot_count, cell_class, class_contrast, background):
    row_index = lax.axis_index("row")
    col_index = lax.axis_index("col")
    stride = lax.axis_size("col")
    slots = green_blocks.shape[2]
    local_rows = slot_rows[0, 0]
    local_cols = slot_cols[0, 0]
    global_rows = local_rows // 2 * stride + 2 * row_index + local_rows % 2
    global_cols = local_cols * stride + col_index
    living = jnp.arange(slots) < slot_count[0, 0]
    row_pick = jnp.where(living & (local_rows == jnp.arange(8)[:, None]), 1.0, 0.0).reshape(-1)
    col_pick = jnp.where(
        living & (global_rows != global_cols) & (local_cols == jnp.arange(4)[:, None]), 1.0, 0.0
    ).reshape(-1)

    classes = class_contrast.shape[0]
    at = cell_class[:, 0, None, :] == jnp.arange(classes)[None, :, None]
    scale = jnp.stack(
        [jnp.sum(jnp.where(at, class_contrast[None, :, part, None], 0.0), axis=1) for part in range(2)]
    )
    scale = jnp.tile(scale, (1, 1, 3))
    lanes = jnp.concatenate(
        [scale[..., :256].reshape(2, 1024), scale[..., 256:].reshape(2, 128)], axis=-1
    ).reshape(2, 3, 384)
    scale = jnp.broadcast_to(lanes.transpose(1, 0, 2)[:, :, None], (3, 2, 8, 384)).reshape(3, 16, 384)
    scale_re, scale_im = lanes[0, :, None], lanes[1, :, None]

    back = pack(background[:, :, :, 0, :])
    pairs = back.reshape(GROUPS, 3, 2, 8, 384)
    re, im = pairs[:, :, 0], pairs[:, :, 1]
    first = (
        jnp.stack([scale_re * re - scale_im * im, scale_re * im + scale_im * re], axis=2)
        .astype(BF16)
        .reshape(SHARDS, 16, 384)
    )

    vmem = pl.BlockSpec(memory_space=pltpu.VMEM)
    smem = pl.BlockSpec(memory_space=pltpu.SMEM)
    packed = (SHARDS, 16, 384)
    steps = (PRODUCTS,)
    dma = pltpu.SemaphoreType.DMA
    field = pl.pallas_call(
        functools.partial(kernel, n_rows),
        out_shape=jax.ShapeDtypeStruct(packed, F32),
        in_specs=[smem] * 4 + [pl.BlockSpec(memory_space=pltpu.HBM)] + [vmem] * 3,
        out_specs=vmem,
        scratch_shapes=[
            pltpu.VMEM(green_blocks.shape[2:], BF16),
            pltpu.VMEM((PRODUCTS - 1,) + packed, BF16),
            pltpu.VMEM((PRODUCTS, 2) + packed, BF16),
            pltpu.VMEM((4, 2, 64, 384), BF16),
            pltpu.VMEM((2, 4, 2, 64, 384), BF16),
            pltpu.VMEM((slots, 64, 384), F32),
            pltpu.VMEM((PRODUCTS, 2) + packed, F32),
            pltpu.VMEM(steps + packed, F32),
            pltpu.VMEM(steps + packed, BF16),
            pltpu.VMEM(steps + packed, BF16),
            pltpu.VMEM((PRODUCTS, 2 * n_rows, 16, 384), BF16),
            pltpu.VMEM((PRODUCTS, 16, 384), BF16),
            pltpu.VMEM((16, 384), F32),
            pltpu.VMEM((2, 16, 384), F32),
            pltpu.VMEM((2, 16, 384), F32),
            dma(()),
            dma((PRODUCTS - 1,)),
            dma(steps),
            dma(steps),
            dma(steps),
            dma(steps),
            dma(()),
            dma(()),
            dma(steps),
            dma(steps),
            dma(steps),
            dma(steps),
            dma(steps),
            dma(()),
            dma(()),
        ],
        compiler_params=pltpu.CompilerParams(
            collective_id=0, has_side_effects=True, vmem_limit_bytes=60 * 2**20
        ),
    )(local_rows, local_cols, row_pick, col_pick, green_blocks, first, back, scale)
    return unpack(field)[:, :, :, None, :]


def solution(mesh):
    in_specs = (
        P("row", "col", None, None, None, None),
        P("row", "col", None),
        P("row", "col", None),
        P("row", "col"),
        P(None, "col", None),
        P(),
        P(None, None, None, "col", None),
    )
    out_specs = P(None, None, None, "col", None)
    return jax.shard_map(
        functools.partial(local, mesh.shape["row"]),
        mesh=mesh,
        in_specs=in_specs,
        out_specs=out_specs,
        check_vma=False,
    )
```

```python
import functools

import jax
import jax.numpy as jnp
from jax import lax
from jax.experimental import pallas as pl
from jax.experimental.pallas import tpu as pltpu
from jax.sharding import PartitionSpec as P

PRODUCTS = 3
SHARDS = 12
TURN = 4
GROUPS = 4
MESH = pl.DeviceIdType.MESH
F32 = jnp.float32
BF16 = jnp.bfloat16
NT = (((1,), (1,)), ((), ()))
NN = (((1,), (0,)), ((), ()))


def pack(field):
    rows = field.reshape(2, GROUPS, 8, 4, 288).transpose(1, 0, 2, 3, 4).reshape(GROUPS, 16, 4, 288)
    main = rows[..., :256].reshape(GROUPS, 16, 1024)
    tail = rows[..., 256:].reshape(GROUPS, 16, 128)
    lanes = jnp.concatenate([main, tail], axis=-1).reshape(GROUPS, 16, 3, 384)
    return lanes.transpose(0, 2, 1, 3).reshape(SHARDS, 16, 384)


def unpack(shards):
    lanes = shards.reshape(GROUPS, 3, 16, 384).transpose(0, 2, 1, 3).reshape(GROUPS, 16, 1152)
    main = lanes[..., :1024].reshape(GROUPS, 16, 4, 256)
    tail = lanes[..., 1024:].reshape(GROUPS, 16, 4, 32)
    rows = jnp.concatenate([main, tail], axis=-1).reshape(GROUPS, 2, 8, 4, 288)
    return rows.transpose(1, 0, 2, 3, 4).reshape(2, 32, 4, 288)


def kernel(
    n_rows,
    rows_ref,
    cols_ref,
    row_pick,
    col_pick,
    g_hbm,
    first_ref,
    back_ref,
    scale_ref,
    out_ref,
    g,
    own,
    across,
    left_own,
    left_across,
    terms,
    half,
    half_in,
    direct,
    mirror,
    arrived,
    now,
    last,
    give,
    given,
    g_sem,
    own_sem,
    across_sem,
    swap_sem,
    half_sem,
    arrived_sem,
    out_sem,
    send_first,
    send_swap,
    send_half,
    send_direct,
    send_mirror,
    send_now,
    given_sem,
    send_given,
):
    slots = g.shape[0]
    r = lax.axis_index("row")
    c = lax.axis_index("col")
    s, k = c // 2, c % 2
    side = n_rows // 4
    diagonal = r == s
    other = (r, 2 * s + 1 - k)

    def turn(row):
        return (row // 2) % TURN

    def place(t):
        return 4 * (t // 3) + t % 3 + (t % 3) // 2 * (t // 3 % 2)

    def seat(h, row):
        return (h // side + turn(row)) % 4 * side + h % side

    hub = (s // side + 4 - turn(r)) % 4 * side + s % side
    reducer = jnp.logical_or(r % 4 < 2, r % 4 == 2 + r // 4 % 2)
    shard = 3 * (r // 4) + jnp.minimum(r % 4, 2)
    in_line = jnp.logical_and(reducer, hub == s)
    in_plane = jnp.logical_and(reducer, hub == r)

    loads = pltpu.make_async_copy(g_hbm.at[0, 0], g, g_sem)
    loads.start()

    barrier = pltpu.get_barrier_semaphore()

    def greet(row, col):
        pl.semaphore_signal(barrier, inc=1, device_id=(row, col), device_id_type=MESH)

    greet(*other)

    def greet_reducers(t, _):
        row = place(t)

        @pl.when(jnp.logical_not(jnp.logical_and(row == r, in_line)))
        def _():
            greet(row, 2 * seat(s, row) + k)

        @pl.when(jnp.logical_not(jnp.logical_and(row == r, in_plane)))
        def _():
            greet(row, 2 * seat(r, row) + k)

        return 0

    lax.fori_loop(0, SHARDS, greet_reducers, 0)

    @pl.when(reducer)
    def _():
        def greet_members(d, _):
            @pl.when(jnp.logical_not(jnp.logical_and(d == r, in_line)))
            def _():
                greet(d, 2 * hub + k)

            @pl.when(jnp.logical_not(jnp.logical_and(d == s, in_plane)))
            def _():
                greet(hub, 2 * d + k)

            return 0

        lax.fori_loop(0, n_rows, greet_members, 0)

    @pl.when(jnp.logical_not(diagonal))
    def _():
        greet(s, 2 * r + k)

    greeted = (
        1
        + jnp.where(diagonal, 0, 1)
        + 2 * SHARDS
        + jnp.where(reducer, 2 * n_rows, 0)
        - jnp.where(in_line, 2, 0)
        - jnp.where(in_plane, 2, 0)
    )

    def send(src, dst, send_sem, recv_sem, row, col):
        pltpu.make_async_remote_copy(
            src_ref=src,
            dst_ref=dst,
            send_sem=send_sem,
            recv_sem=recv_sem,
            device_id=(row, col),
            device_id_type=MESH,
        ).start()

    def take(ref, sem):
        pltpu.make_async_copy(ref, ref, sem).wait()

    def spread(src, dst, send_sem, recv_sem, d):
        mine = jnp.logical_and(d == r, in_line)

        @pl.when(mine)
        def _():
            pltpu.make_async_copy(src, dst, recv_sem).start()

        @pl.when(jnp.logical_not(mine))
        def _():
            send(src, dst, send_sem, recv_sem, d, 2 * hub + k)

    def unfold(packed, lefts):
        def group(i, _):
            at = pl.ds(pl.multiple_of(16 * i, 16), 16)

            def put(q, lane, value):
                turned = jnp.concatenate([-value[8:], value[:8]], axis=0)
                lefts[q, 0, at, lane : lane + 128] = value.astype(BF16)
                lefts[q, 1, at, lane : lane + 128] = turned.astype(BF16)

            for tile in range(8):
                value = packed[3 * i + tile // 3, :, 128 * (tile % 3) : 128 * (tile % 3) + 128]
                put(tile // 2, 128 * (tile % 2), value.astype(F32))
            tail = packed[3 * i + 2, :, 256:384].astype(F32)
            put(0, 256, tail)
            for q in range(1, 4):
                put(q, 256, pltpu.roll(tail, 128 - 32 * q, 1))
            return 0

        lax.fori_loop(0, GROUPS, group, 0, unroll=True)

    def products(lefts, picks, dims):
        def one(slot, _):
            at = picks[slot]
            re = lefts[at, 0, :, :288]
            im = lefts[at, 1, :, :288]
            terms[slot, :, :288] = lax.dot_general(
                re, g[slot, 0], dims, preferred_element_type=F32
            ) + lax.dot_general(im, g[slot, 1], dims, preferred_element_type=F32)
            return 0

        lax.fori_loop(0, slots, one, 0, unroll=slots)

    def gather_terms(pick, first, step, out, after=None):
        def group(i, _):
            at = pl.ds(pl.multiple_of(16 * i, 16), 16)
            tail = None
            for q in range(4):
                total = None
                for slot in range(slots):
                    value = terms[slot, at, :] * pick[(first + step * q) * slots + slot]
                    total = value if total is None else total + value
                for part in range(2):
                    tile = 2 * q + part
                    out[3 * i + tile // 3, :, 128 * (tile % 3) : 128 * (tile % 3) + 128] = total[
                        :, 128 * part : 128 * part + 128
                    ].astype(out.dtype)
                last = total[:, 256:384]
                last = pltpu.roll(last, 32 * q, 1) if q else last
                tail = last if tail is None else tail + last
            out[3 * i + 2, :, 256:384] = tail.astype(out.dtype)
            if after is not None:
                after(i)
            return 0

        lax.fori_loop(0, GROUPS, group, 0, unroll=True)

    terms[:, :, 256:384] = jnp.zeros((slots, 64, 128), F32)
    unfold(first_ref, left_own)

    pl.semaphore_wait(barrier, greeted)

    @pl.when(jnp.logical_not(diagonal))
    def _():
        send(first_ref, across.at[0, k], send_first, across_sem.at[0], s, 2 * r + k)

    @pl.when(diagonal)
    def _():
        pltpu.make_async_copy(first_ref, across.at[0, k], across_sem.at[0]).start()

    @pl.when(reducer)
    def _():
        give[0] = back_ref[shard]
        give[1] = scale_ref[shard % 3]

        @pl.when(in_line)
        def _():
            pltpu.make_async_copy(give, given, given_sem).start()

        @pl.when(jnp.logical_not(in_line))
        def _():
            send(give, given, send_given, given_sem, r, 2 * seat(s, r) + k)

    loads.wait()

    def update(step, final):
        products(left_own, cols_ref, NT)
        def send_half_group(i):
            part = pl.ds(3 * i, 3)
            send(half.at[step, 1, part], half_in.at[step, part], send_half.at[step], half_sem.at[step], *other)

        gather_terms(row_pick, 1 - k, 2, half.at[step, 1], send_half_group)
        gather_terms(row_pick, k, 2, half.at[step, 0])

        take(half_in.at[step], half_sem.at[step])

        def send_one(t, _):
            direct[step, t] = (half[step, 0, t] + half_in[step, t]).astype(BF16)
            row = place(t)
            mine = jnp.logical_and(row == r, in_plane)
            dst = arrived.at[step, s]

            @pl.when(mine)
            def _():
                pltpu.make_async_copy(direct.at[step, t], dst, arrived_sem.at[step]).start()

            @pl.when(jnp.logical_not(mine))
            def _():
                send(direct.at[step, t], dst, send_direct.at[step], arrived_sem.at[step], row, 2 * seat(r, row) + k)

            return 0

        lax.fori_loop(0, SHARDS, send_one, 0)

        take(across.at[step, k], across_sem.at[step])
        send(across.at[step, k], across.at[step, k], send_swap.at[step], swap_sem.at[step], *other)
        unfold(across.at[step, k], left_across.at[k])
        take(across.at[step, 1 - k], swap_sem.at[step])
        unfold(across.at[step, 1 - k], left_across.at[1 - k])
        products_across()
        def send_mine(t, _):
            row = place(t)
            mine = jnp.logical_and(row == r, in_line)
            dst = arrived.at[step, n_rows + r]

            @pl.when(mine)
            def _():
                pltpu.make_async_copy(mirror.at[step, t], dst, arrived_sem.at[step]).start()

            @pl.when(jnp.logical_not(mine))
            def _():
                send(mirror.at[step, t], dst, send_mirror.at[step], arrived_sem.at[step], row, 2 * seat(s, row) + k)

            return 0

        def send_mine_group(i):
            for part in range(3):
                send_mine(3 * i + part, 0)

        gather_terms(col_pick, 0, 1, mirror.at[step], send_mine_group)

        @pl.when(reducer)
        def _():
            take(arrived.at[step], arrived_sem.at[step])

            def add(j, total):
                return total + arrived[step, j].astype(F32)


            @pl.when(step == 0)
            def _():
                take(given, given_sem)

            field = lax.fori_loop(0, 2 * n_rows, add, given[0], unroll=8)
            if final:
                last[...] = field
            else:
                re, im = field[:8], field[8:]
                scale_re, scale_im = given[1, :8], given[1, 8:]
                now[step, :8] = (scale_re * re - scale_im * im).astype(BF16)
                now[step, 8:] = (scale_re * im + scale_im * re).astype(BF16)

        if final:
            return

        @pl.when(reducer)
        def _():
            src = now.at[step]
            line = own.at[step, shard]
            plane = across.at[step + 1, k, shard]

            def spread_line(d, _):
                spread(src, line, send_now.at[step], own_sem.at[step], d)
                return 0

            lax.fori_loop(0, n_rows, spread_line, 0)

            def spread_plane(d, _):
                mine = jnp.logical_and(d == s, in_plane)

                @pl.when(mine)
                def _():
                    pltpu.make_async_copy(src, plane, across_sem.at[step + 1]).start()

                @pl.when(jnp.logical_not(mine))
                def _():
                    send(src, plane, send_now.at[step], across_sem.at[step + 1], hub, 2 * d + k)

                return 0

            lax.fori_loop(0, n_rows, spread_plane, 0)

        take(own.at[step], own_sem.at[step])
        unfold(own.at[step], left_own)

    def products_across():
        def one(slot, _):
            at = rows_ref[slot]
            re = left_across[at % 2, at // 2, 0, :, :288]
            im = left_across[at % 2, at // 2, 1, :, :288]
            terms[slot, :, :288] = lax.dot_general(
                re, g[slot, 0], NN, preferred_element_type=F32
            ) + lax.dot_general(im, g[slot, 1], NN, preferred_element_type=F32)
            return 0

        lax.fori_loop(0, slots, one, 0, unroll=slots)

    def early(step, _):
        update(step, False)
        return 0

    lax.fori_loop(0, PRODUCTS - 1, early, 0)
    update(PRODUCTS - 1, True)

    @pl.when(reducer)
    def _():
        def spread_last(d, _):
            spread(last, out_ref.at[shard], send_now.at[PRODUCTS - 1], out_sem, d)
            return 0

        lax.fori_loop(0, n_rows, spread_last, 0)

    take(out_ref, out_sem)

    @pl.when(in_line)
    def _():
        take(arrived.at[0, pl.ds(0, 2 * n_rows - 2)], send_now.at[PRODUCTS - 1])

    @pl.when(jnp.logical_and(reducer, hub != s))
    def _():
        take(arrived.at[0], send_now.at[PRODUCTS - 1])
        take(given, send_given)

    @pl.when(jnp.logical_not(diagonal))
    def _():
        take(first_ref, send_first)

    def finish(step, _):
        take(across.at[step, 0], send_swap.at[step])
        take(half_in.at[step], send_half.at[step])

        def sent(ref, less, send_sem):
            @pl.when(less)
            def _():
                take(ref.at[pl.ds(0, SHARDS - 1)], send_sem)

            @pl.when(jnp.logical_not(less))
            def _():
                take(ref, send_sem)

        sent(direct.at[step], in_plane, send_direct.at[step])
        sent(mirror.at[step], in_line, send_mirror.at[step])

        @pl.when(jnp.logical_and(reducer, step < PRODUCTS - 1))
        def _():
            both = jnp.logical_and(in_line, in_plane)
            either = jnp.logical_or(in_line, in_plane)

            @pl.when(both)
            def _():
                take(arrived.at[step, pl.ds(0, 2 * n_rows - 2)], send_now.at[step])

            @pl.when(jnp.logical_and(either, jnp.logical_not(both)))
            def _():
                take(arrived.at[step, pl.ds(0, 2 * n_rows - 1)], send_now.at[step])

            @pl.when(jnp.logical_not(either))
            def _():
                take(arrived.at[step], send_now.at[step])

        return 0

    lax.fori_loop(0, PRODUCTS, finish, 0)


def local(n_rows, green_blocks, slot_rows, slot_cols, slot_count, cell_class, class_contrast, background):
    row_index = lax.axis_index("row")
    col_index = lax.axis_index("col")
    stride = lax.axis_size("col")
    slots = green_blocks.shape[2]
    local_rows = slot_rows[0, 0]
    local_cols = slot_cols[0, 0]
    global_rows = local_rows // 2 * stride + 2 * row_index + local_rows % 2
    global_cols = local_cols * stride + col_index
    living = jnp.arange(slots) < slot_count[0, 0]
    row_pick = jnp.where(living & (local_rows == jnp.arange(8)[:, None]), 1.0, 0.0).reshape(-1)
    col_pick = jnp.where(
        living & (global_rows != global_cols) & (local_cols == jnp.arange(4)[:, None]), 1.0, 0.0
    ).reshape(-1)

    classes = class_contrast.shape[0]
    at = cell_class[:, 0, None, :] == jnp.arange(classes)[None, :, None]
    scale = jnp.stack(
        [jnp.sum(jnp.where(at, class_contrast[None, :, part, None], 0.0), axis=1) for part in range(2)]
    )
    scale = jnp.tile(scale, (1, 1, 3))
    lanes = jnp.concatenate(
        [scale[..., :256].reshape(2, 1024), scale[..., 256:].reshape(2, 128)], axis=-1
    ).reshape(2, 3, 384)
    scale = jnp.broadcast_to(lanes.transpose(1, 0, 2)[:, :, None], (3, 2, 8, 384)).reshape(3, 16, 384)
    scale_re, scale_im = lanes[0, :, None], lanes[1, :, None]

    back = pack(background[:, :, :, 0, :])
    pairs = back.reshape(GROUPS, 3, 2, 8, 384)
    re, im = pairs[:, :, 0], pairs[:, :, 1]
    first = (
        jnp.stack([scale_re * re - scale_im * im, scale_re * im + scale_im * re], axis=2)
        .astype(BF16)
        .reshape(SHARDS, 16, 384)
    )

    vmem = pl.BlockSpec(memory_space=pltpu.VMEM)
    smem = pl.BlockSpec(memory_space=pltpu.SMEM)
    packed = (SHARDS, 16, 384)
    steps = (PRODUCTS,)
    dma = pltpu.SemaphoreType.DMA
    field = pl.pallas_call(
        functools.partial(kernel, n_rows),
        out_shape=jax.ShapeDtypeStruct(packed, F32),
        in_specs=[smem] * 4 + [pl.BlockSpec(memory_space=pltpu.HBM)] + [vmem] * 3,
        out_specs=vmem,
        scratch_shapes=[
            pltpu.VMEM(green_blocks.shape[2:], BF16),
            pltpu.VMEM((PRODUCTS - 1,) + packed, BF16),
            pltpu.VMEM((PRODUCTS, 2) + packed, BF16),
            pltpu.VMEM((4, 2, 64, 384), BF16),
            pltpu.VMEM((2, 4, 2, 64, 384), BF16),
            pltpu.VMEM((slots, 64, 384), F32),
            pltpu.VMEM((PRODUCTS, 2) + packed, F32),
            pltpu.VMEM(steps + packed, F32),
            pltpu.VMEM(steps + packed, BF16),
            pltpu.VMEM(steps + packed, BF16),
            pltpu.VMEM((PRODUCTS, 2 * n_rows, 16, 384), BF16),
            pltpu.VMEM((PRODUCTS, 16, 384), BF16),
            pltpu.VMEM((16, 384), F32),
            pltpu.VMEM((2, 16, 384), F32),
            pltpu.VMEM((2, 16, 384), F32),
            dma(()),
            dma((PRODUCTS - 1,)),
            dma(steps),
            dma(steps),
            dma(steps),
            dma(steps),
            dma(()),
            dma(()),
            dma(steps),
            dma(steps),
            dma(steps),
            dma(steps),
            dma(steps),
            dma(()),
            dma(()),
        ],
        compiler_params=pltpu.CompilerParams(
            collective_id=0, has_side_effects=True, vmem_limit_bytes=32 * 2**20
        ),
    )(local_rows, local_cols, row_pick, col_pick, green_blocks, first, back, scale)
    return unpack(field)[:, :, :, None, :]


def solution(mesh):
    in_specs = (
        P("row", "col", None, None, None, None),
        P("row", "col", None),
        P("row", "col", None),
        P("row", "col"),
        P(None, "col", None),
        P(),
        P(None, None, None, "col", None),
    )
    out_specs = P(None, None, None, "col", None)
    return jax.shard_map(
        functools.partial(local, mesh.shape["row"]),
        mesh=mesh,
        in_specs=in_specs,
        out_specs=out_specs,
        check_vma=False,
    )
```

```python
import functools

import jax
import jax.numpy as jnp
from jax import lax
from jax.experimental import pallas as pl
from jax.experimental.pallas import tpu as pltpu
from jax.sharding import PartitionSpec as P

PRODUCTS = 3
SHARDS = 12
TURN = 4
GROUPS = 4
MESH = pl.DeviceIdType.MESH
F32 = jnp.float32
BF16 = jnp.bfloat16
NT = (((1,), (1,)), ((), ()))
NN = (((1,), (0,)), ((), ()))


def pack(field):
    rows = field.reshape(2, GROUPS, 8, 4, 288).transpose(1, 0, 2, 3, 4).reshape(GROUPS, 16, 4, 288)
    main = rows[..., :256].reshape(GROUPS, 16, 1024)
    tail = rows[..., 256:].reshape(GROUPS, 16, 128)
    lanes = jnp.concatenate([main, tail], axis=-1).reshape(GROUPS, 16, 3, 384)
    return lanes.transpose(0, 2, 1, 3).reshape(SHARDS, 16, 384)


def unpack(shards):
    lanes = shards.reshape(GROUPS, 3, 16, 384).transpose(0, 2, 1, 3).reshape(GROUPS, 16, 1152)
    main = lanes[..., :1024].reshape(GROUPS, 16, 4, 256)
    tail = lanes[..., 1024:].reshape(GROUPS, 16, 4, 32)
    rows = jnp.concatenate([main, tail], axis=-1).reshape(GROUPS, 2, 8, 4, 288)
    return rows.transpose(1, 0, 2, 3, 4).reshape(2, 32, 4, 288)


def kernel(
    n_rows,
    rows_ref,
    cols_ref,
    row_pick,
    col_pick,
    g_hbm,
    first_ref,
    back_ref,
    scale_ref,
    out_ref,
    g,
    own,
    across,
    left_own,
    left_across,
    terms,
    half,
    half_in,
    direct,
    mirror,
    arrived,
    now,
    last,
    give,
    given,
    g_sem,
    own_sem,
    across_sem,
    swap_sem,
    half_sem,
    arrived_sem,
    out_sem,
    send_first,
    send_swap,
    send_half,
    send_direct,
    send_mirror,
    send_now,
    given_sem,
    send_given,
):
    slots = g.shape[0]
    r = lax.axis_index("row")
    c = lax.axis_index("col")
    s, k = c // 2, c % 2
    side = n_rows // 4
    diagonal = r == s
    other = (r, 2 * s + 1 - k)

    def turn(row):
        return (row // 2) % TURN

    def place(t):
        return 4 * (t // 3) + t % 3 + (t % 3) // 2 * (t // 3 % 2)

    def seat(h, row):
        return (h // side + turn(row)) % 4 * side + h % side

    hub = (s // side + 4 - turn(r)) % 4 * side + s % side
    reducer = jnp.logical_or(r % 4 < 2, r % 4 == 2 + r // 4 % 2)
    shard = 3 * (r // 4) + jnp.minimum(r % 4, 2)
    in_line = jnp.logical_and(reducer, hub == s)
    in_plane = jnp.logical_and(reducer, hub == r)

    loads = pltpu.make_async_copy(g_hbm.at[0, 0], g, g_sem)
    loads.start()

    barrier = pltpu.get_barrier_semaphore()

    def greet(row, col):
        pl.semaphore_signal(barrier, inc=1, device_id=(row, col), device_id_type=MESH)

    greet(*other)

    def greet_reducers(t, _):
        row = place(t)

        @pl.when(jnp.logical_not(jnp.logical_and(row == r, in_line)))
        def _():
            greet(row, 2 * seat(s, row) + k)

        @pl.when(jnp.logical_not(jnp.logical_and(row == r, in_plane)))
        def _():
            greet(row, 2 * seat(r, row) + k)

        return 0

    lax.fori_loop(0, SHARDS, greet_reducers, 0)

    @pl.when(reducer)
    def _():
        def greet_members(d, _):
            @pl.when(jnp.logical_not(jnp.logical_and(d == r, in_line)))
            def _():
                greet(d, 2 * hub + k)

            @pl.when(jnp.logical_not(jnp.logical_and(d == s, in_plane)))
            def _():
                greet(hub, 2 * d + k)

            return 0

        lax.fori_loop(0, n_rows, greet_members, 0)

    @pl.when(jnp.logical_not(diagonal))
    def _():
        greet(s, 2 * r + k)

    greeted = (
        1
        + jnp.where(diagonal, 0, 1)
        + 2 * SHARDS
        + jnp.where(reducer, 2 * n_rows, 0)
        - jnp.where(in_line, 2, 0)
        - jnp.where(in_plane, 2, 0)
    )

    def send(src, dst, send_sem, recv_sem, row, col):
        pltpu.make_async_remote_copy(
            src_ref=src,
            dst_ref=dst,
            send_sem=send_sem,
            recv_sem=recv_sem,
            device_id=(row, col),
            device_id_type=MESH,
        ).start()

    def take(ref, sem):
        pltpu.make_async_copy(ref, ref, sem).wait()

    def spread(src, dst, send_sem, recv_sem, d):
        mine = jnp.logical_and(d == r, in_line)

        @pl.when(mine)
        def _():
            pltpu.make_async_copy(src, dst, recv_sem).start()

        @pl.when(jnp.logical_not(mine))
        def _():
            send(src, dst, send_sem, recv_sem, d, 2 * hub + k)

    def unfold(packed, lefts):
        def group(i, _):
            at = pl.ds(pl.multiple_of(16 * i, 16), 16)

            def put(q, lane, value):
                turned = jnp.concatenate([-value[8:], value[:8]], axis=0)
                lefts[q, 0, at, lane : lane + 128] = value.astype(BF16)
                lefts[q, 1, at, lane : lane + 128] = turned.astype(BF16)

            for tile in range(8):
                value = packed[3 * i + tile // 3, :, 128 * (tile % 3) : 128 * (tile % 3) + 128]
                put(tile // 2, 128 * (tile % 2), value.astype(F32))
            tail = packed[3 * i + 2, :, 256:384].astype(F32)
            put(0, 256, tail)
            for q in range(1, 4):
                put(q, 256, pltpu.roll(tail, 128 - 32 * q, 1))
            return 0

        lax.fori_loop(0, GROUPS, group, 0, unroll=True)

    def products(lefts, picks, dims):
        def one(slot, _):
            at = picks[slot]
            re = lefts[at, 0, :, :288]
            im = lefts[at, 1, :, :288]
            terms[slot, :, :288] = lax.dot_general(
                re, g[slot, 0], dims, preferred_element_type=F32
            ) + lax.dot_general(im, g[slot, 1], dims, preferred_element_type=F32)
            return 0

        lax.fori_loop(0, slots, one, 0, unroll=slots)

    def gather_terms(pick, first, step, out, after=None, start=None):
        def group(i, _):
            i = i if start is None else (i + start) % GROUPS
            at = pl.ds(pl.multiple_of(16 * i, 16), 16)
            tail = None
            for q in range(4):
                total = None
                for slot in range(slots):
                    value = terms[slot, at, :] * pick[(first + step * q) * slots + slot]
                    total = value if total is None else total + value
                for part in range(2):
                    tile = 2 * q + part
                    out[3 * i + tile // 3, :, 128 * (tile % 3) : 128 * (tile % 3) + 128] = total[
                        :, 128 * part : 128 * part + 128
                    ].astype(out.dtype)
                last = total[:, 256:384]
                last = pltpu.roll(last, 32 * q, 1) if q else last
                tail = last if tail is None else tail + last
            out[3 * i + 2, :, 256:384] = tail.astype(out.dtype)
            if after is not None:
                after(i)
            return 0

        lax.fori_loop(0, GROUPS, group, 0, unroll=True)

    terms[:, :, 256:384] = jnp.zeros((slots, 64, 128), F32)
    unfold(first_ref, left_own)

    pl.semaphore_wait(barrier, greeted)

    @pl.when(jnp.logical_not(diagonal))
    def _():
        send(first_ref, across.at[0, k], send_first, across_sem.at[0], s, 2 * r + k)

    @pl.when(diagonal)
    def _():
        pltpu.make_async_copy(first_ref, across.at[0, k], across_sem.at[0]).start()

    @pl.when(reducer)
    def _():
        give[0] = back_ref[shard]
        give[1] = scale_ref[shard % 3]

        @pl.when(in_line)
        def _():
            pltpu.make_async_copy(give, given, given_sem).start()

        @pl.when(jnp.logical_not(in_line))
        def _():
            send(give, given, send_given, given_sem, r, 2 * seat(s, r) + k)

    loads.wait()

    def update(step, final):
        products(left_own, cols_ref, NT)

        def send_half_group(i):
            part = pl.ds(3 * i, 3)
            send(half.at[step, 1, part], half_in.at[step, part], send_half.at[step], half_sem.at[step], *other)

        gather_terms(row_pick, 1 - k, 2, half.at[step, 1], send_half_group)
        gather_terms(row_pick, k, 2, half.at[step, 0])

        take(half_in.at[step], half_sem.at[step])

        def send_one(t, _):
            t = (t + s) % SHARDS
            direct[step, t] = (half[step, 0, t] + half_in[step, t]).astype(BF16)
            row = place(t)
            mine = jnp.logical_and(row == r, in_plane)
            dst = arrived.at[step, s]

            @pl.when(mine)
            def _():
                pltpu.make_async_copy(direct.at[step, t], dst, arrived_sem.at[step]).start()

            @pl.when(jnp.logical_not(mine))
            def _():
                send(direct.at[step, t], dst, send_direct.at[step], arrived_sem.at[step], row, 2 * seat(r, row) + k)

            return 0

        lax.fori_loop(0, SHARDS, send_one, 0)

        take(across.at[step, k], across_sem.at[step])
        send(across.at[step, k], across.at[step, k], send_swap.at[step], swap_sem.at[step], *other)
        unfold(across.at[step, k], left_across.at[k])
        take(across.at[step, 1 - k], swap_sem.at[step])
        unfold(across.at[step, 1 - k], left_across.at[1 - k])
        products_across()

        def send_mine(t, _):
            row = place(t)
            mine = jnp.logical_and(row == r, in_line)
            dst = arrived.at[step, n_rows + r]

            @pl.when(mine)
            def _():
                pltpu.make_async_copy(mirror.at[step, t], dst, arrived_sem.at[step]).start()

            @pl.when(jnp.logical_not(mine))
            def _():
                send(mirror.at[step, t], dst, send_mirror.at[step], arrived_sem.at[step], row, 2 * seat(s, row) + k)

            return 0

        def send_mine_group(i):
            for part in range(3):
                send_mine(3 * i + part, 0)

        gather_terms(col_pick, 0, 1, mirror.at[step], send_mine_group, r)

        @pl.when(reducer)
        def _():
            take(arrived.at[step], arrived_sem.at[step])

            def add(j, total):
                return total + arrived[step, j].astype(F32)


            @pl.when(step == 0)
            def _():
                take(given, given_sem)

            field = lax.fori_loop(0, 2 * n_rows, add, given[0], unroll=8)
            if final:
                last[...] = field
            else:
                re, im = field[:8], field[8:]
                scale_re, scale_im = given[1, :8], given[1, 8:]
                now[step, :8] = (scale_re * re - scale_im * im).astype(BF16)
                now[step, 8:] = (scale_re * im + scale_im * re).astype(BF16)

        if final:
            return

        @pl.when(reducer)
        def _():
            src = now.at[step]
            line = own.at[step, shard]
            plane = across.at[step + 1, k, shard]

            def spread_line(d, _):
                spread(src, line, send_now.at[step], own_sem.at[step], (r + d) % n_rows)
                return 0

            lax.fori_loop(0, n_rows, spread_line, 0)

            def spread_plane(d, _):
                seat_d = (s + d) % n_rows
                mine = jnp.logical_and(seat_d == s, in_plane)

                @pl.when(mine)
                def _():
                    pltpu.make_async_copy(src, plane, across_sem.at[step + 1]).start()

                @pl.when(jnp.logical_not(mine))
                def _():
                    send(src, plane, send_now.at[step], across_sem.at[step + 1], hub, 2 * seat_d + k)

                return 0

            lax.fori_loop(0, n_rows, spread_plane, 0)

        take(own.at[step], own_sem.at[step])
        unfold(own.at[step], left_own)

    def products_across():
        def one(slot, _):
            at = rows_ref[slot]
            re = left_across[at % 2, at // 2, 0, :, :288]
            im = left_across[at % 2, at // 2, 1, :, :288]
            terms[slot, :, :288] = lax.dot_general(
                re, g[slot, 0], NN, preferred_element_type=F32
            ) + lax.dot_general(im, g[slot, 1], NN, preferred_element_type=F32)
            return 0

        lax.fori_loop(0, slots, one, 0, unroll=slots)

    def early(step, _):
        update(step, False)
        return 0

    lax.fori_loop(0, PRODUCTS - 1, early, 0)
    update(PRODUCTS - 1, True)

    @pl.when(reducer)
    def _():
        def spread_last(d, _):
            spread(last, out_ref.at[shard], send_now.at[PRODUCTS - 1], out_sem, (r + d) % n_rows)
            return 0

        lax.fori_loop(0, n_rows, spread_last, 0)

    take(out_ref, out_sem)

    @pl.when(in_line)
    def _():
        take(arrived.at[0, pl.ds(0, 2 * n_rows - 2)], send_now.at[PRODUCTS - 1])

    @pl.when(jnp.logical_and(reducer, hub != s))
    def _():
        take(arrived.at[0], send_now.at[PRODUCTS - 1])
        take(given, send_given)

    @pl.when(jnp.logical_not(diagonal))
    def _():
        take(first_ref, send_first)

    def finish(step, _):
        take(across.at[step, 0], send_swap.at[step])
        take(half_in.at[step], send_half.at[step])

        def sent(ref, less, send_sem):
            @pl.when(less)
            def _():
                take(ref.at[pl.ds(0, SHARDS - 1)], send_sem)

            @pl.when(jnp.logical_not(less))
            def _():
                take(ref, send_sem)

        sent(direct.at[step], in_plane, send_direct.at[step])
        sent(mirror.at[step], in_line, send_mirror.at[step])

        @pl.when(jnp.logical_and(reducer, step < PRODUCTS - 1))
        def _():
            both = jnp.logical_and(in_line, in_plane)
            either = jnp.logical_or(in_line, in_plane)

            @pl.when(both)
            def _():
                take(arrived.at[step, pl.ds(0, 2 * n_rows - 2)], send_now.at[step])

            @pl.when(jnp.logical_and(either, jnp.logical_not(both)))
            def _():
                take(arrived.at[step, pl.ds(0, 2 * n_rows - 1)], send_now.at[step])

            @pl.when(jnp.logical_not(either))
            def _():
                take(arrived.at[step], send_now.at[step])

        return 0

    lax.fori_loop(0, PRODUCTS, finish, 0)


def local(n_rows, green_blocks, slot_rows, slot_cols, slot_count, cell_class, class_contrast, background):
    row_index = lax.axis_index("row")
    col_index = lax.axis_index("col")
    stride = lax.axis_size("col")
    slots = green_blocks.shape[2]
    local_rows = slot_rows[0, 0]
    local_cols = slot_cols[0, 0]
    global_rows = local_rows // 2 * stride + 2 * row_index + local_rows % 2
    global_cols = local_cols * stride + col_index
    living = jnp.arange(slots) < slot_count[0, 0]
    row_pick = jnp.where(living & (local_rows == jnp.arange(8)[:, None]), 1.0, 0.0).reshape(-1)
    col_pick = jnp.where(
        living & (global_rows != global_cols) & (local_cols == jnp.arange(4)[:, None]), 1.0, 0.0
    ).reshape(-1)

    classes = class_contrast.shape[0]
    at = cell_class[:, 0, None, :] == jnp.arange(classes)[None, :, None]
    scale = jnp.stack(
        [jnp.sum(jnp.where(at, class_contrast[None, :, part, None], 0.0), axis=1) for part in range(2)]
    )
    scale = jnp.tile(scale, (1, 1, 3))
    lanes = jnp.concatenate(
        [scale[..., :256].reshape(2, 1024), scale[..., 256:].reshape(2, 128)], axis=-1
    ).reshape(2, 3, 384)
    scale = jnp.broadcast_to(lanes.transpose(1, 0, 2)[:, :, None], (3, 2, 8, 384)).reshape(3, 16, 384)
    scale_re, scale_im = lanes[0, :, None], lanes[1, :, None]

    back = pack(background[:, :, :, 0, :])
    pairs = back.reshape(GROUPS, 3, 2, 8, 384)
    re, im = pairs[:, :, 0], pairs[:, :, 1]
    first = (
        jnp.stack([scale_re * re - scale_im * im, scale_re * im + scale_im * re], axis=2)
        .astype(BF16)
        .reshape(SHARDS, 16, 384)
    )

    vmem = pl.BlockSpec(memory_space=pltpu.VMEM)
    smem = pl.BlockSpec(memory_space=pltpu.SMEM)
    packed = (SHARDS, 16, 384)
    steps = (PRODUCTS,)
    dma = pltpu.SemaphoreType.DMA
    field = pl.pallas_call(
        functools.partial(kernel, n_rows),
        out_shape=jax.ShapeDtypeStruct(packed, F32),
        in_specs=[smem] * 4 + [pl.BlockSpec(memory_space=pltpu.HBM)] + [vmem] * 3,
        out_specs=vmem,
        scratch_shapes=[
            pltpu.VMEM(green_blocks.shape[2:], BF16),
            pltpu.VMEM((PRODUCTS - 1,) + packed, BF16),
            pltpu.VMEM((PRODUCTS, 2) + packed, BF16),
            pltpu.VMEM((4, 2, 64, 384), BF16),
            pltpu.VMEM((2, 4, 2, 64, 384), BF16),
            pltpu.VMEM((slots, 64, 384), F32),
            pltpu.VMEM((PRODUCTS, 2) + packed, F32),
            pltpu.VMEM(steps + packed, F32),
            pltpu.VMEM(steps + packed, BF16),
            pltpu.VMEM(steps + packed, BF16),
            pltpu.VMEM((PRODUCTS, 2 * n_rows, 16, 384), BF16),
            pltpu.VMEM((PRODUCTS, 16, 384), BF16),
            pltpu.VMEM((16, 384), F32),
            pltpu.VMEM((2, 16, 384), F32),
            pltpu.VMEM((2, 16, 384), F32),
            dma(()),
            dma((PRODUCTS - 1,)),
            dma(steps),
            dma(steps),
            dma(steps),
            dma(steps),
            dma(()),
            dma(()),
            dma(steps),
            dma(steps),
            dma(steps),
            dma(steps),
            dma(steps),
            dma(()),
            dma(()),
        ],
        compiler_params=pltpu.CompilerParams(
            collective_id=0, has_side_effects=True, vmem_limit_bytes=32 * 2**20
        ),
    )(local_rows, local_cols, row_pick, col_pick, green_blocks, first, back, scale)
    return unpack(field)[:, :, :, None, :]


def solution(mesh):
    in_specs = (
        P("row", "col", None, None, None, None),
        P("row", "col", None),
        P("row", "col", None),
        P("row", "col"),
        P(None, "col", None),
        P(),
        P(None, None, None, "col", None),
    )
    out_specs = P(None, None, None, "col", None)
    return jax.shard_map(
        functools.partial(local, mesh.shape["row"]),
        mesh=mesh,
        in_specs=in_specs,
        out_specs=out_specs,
        check_vma=False,
    )
```
